512 devices in a mesh: dp: 16 (over z_lo, y), tensor: 32 (over x, z_hi, core).
Axes of the slice: x: 4, y: 4, z: 16 (z_hi: 4, z_lo: 4; z = z_hi * 4 + z_lo), core: 2. Of those that a mesh axis runs over, the one named last changes fastest.
Arguments:
- tokens_in: bfloat16 [16384, 8192], P('dp', 'tensor'), may hold values from -6 to 6
- out_grad: bfloat16 [16384, 8192], P('dp', 'tensor'), may hold values from -6 to 6
- left_up: bfloat16 [8192, 256], P('tensor'), may hold values from -0.375 to 0.375
- right_up: bfloat16 [8192, 1024], P('tensor'), may hold values from -0.375 to 0.375
- left_down: bfloat16 [32768, 256], P('tensor'), may hold values from -0.1875 to 0.1875
- right_down: bfloat16 [8192, 256], P('tensor'), may hold values from -0.375 to 0.375
Outputs:
- layer_out: bfloat16 [16384, 8192], P('dp', 'tensor')
- input_grad: bfloat16 [16384, 8192], P('dp', 'tensor')
- grad_left_up: bfloat16 [8192, 256], P('tensor')
- grad_right_up: bfloat16 [8192, 1024], P('tensor')
- grad_left_down: bfloat16 [32768, 256], P('tensor')
- grad_right_down: bfloat16 [8192, 256], P('tensor')
The draws below stay inside these ranges and needn't reach their ends.
All inputs are finite; a program needn't handle non-finite values.
Results may differ from the reference program's by a relative error of at most 0.0075.
Values may be sent and summed in bfloat16 or wider, within the bound.
No kernel may reach another device: no remote copies, remote signals or barrier semaphores. Data moves between devices by JAX's collectives and lax.ppermute only.
A program may use at most 64 MiB of HBM per device.

```python
import jax
import jax.numpy as jnp

D = 8192
FF = 32768
BLOCKS = 32
BLK = 256
FBLK = 1024
TOKENS = 16384


def steps_of(key, extent, pieces, smallest, largest):
    level, own = 1.0, jax.random.fold_in(key, 6)
    for dim, parts in pieces:
        draws = jnp.exp(jax.random.uniform(jax.random.fold_in(own, dim), (parts,), jnp.float32, smallest / len(pieces), largest / len(pieces)))
        level = level * jnp.repeat(draws, extent[dim] // parts).reshape([-1 if axis == dim else 1 for axis in range(len(extent))])
    return level


def normal_values(own_key, shape, width, bound, split=(), kind=jnp.bfloat16):
    values = jax.random.normal(own_key, shape, jnp.float32) * width
    if len(split) > 0:
        values = steps_of(own_key, shape, split, -0.22, 0.18) * values
    return jnp.clip(values, min=-bound, max=bound).astype(kind)


def setup_inputs(seed: int = 0) -> dict:
    splits = jax.random.split(jax.random.key(seed), 7)
    tokens_in = normal_values(splits[0], (TOKENS, D), 1.0, 6.0, ((0, 16), (1, 32)))
    out_grad = normal_values(splits[1], (TOKENS, D), 1.0, 6.0, ((0, 16), (1, 32)))
    left_up = normal_values(splits[2], (D, BLK), BLK ** -0.5, 0.375, ((0, 32),))
    right_up = normal_values(splits[3], (D, FBLK), BLK ** -0.5, 0.375, ((0, 32),))
    left_down = normal_values(splits[4], (FF, BLK), FBLK ** -0.5, 0.1875, ((0, 32),))
    right_down = normal_values(splits[5], (D, BLK), BLK ** -0.5, 0.375, ((0, 32),))
    return dict(tokens_in=tokens_in, out_grad=out_grad, left_up=left_up, right_up=right_up, left_down=left_down, right_down=right_down)


def permute(values):
    count = values.shape[0]
    sub = BLK // BLOCKS
    return values.reshape(count, BLOCKS, BLOCKS, sub).transpose(0, 2, 1, 3).reshape(count, -1)

def blockdot(values, weights, width_in, width_out):
    count = values.shape[0]
    left = values.reshape(count, BLOCKS, width_in).astype(jnp.float32)
    right = weights.reshape(BLOCKS, width_in, width_out).astype(jnp.float32)
    return jnp.einsum('nbk,bkc->nbc', left, right).reshape(count, BLOCKS * width_out)

def blockdot_t(grads, weights, width_in, width_out):
    count = grads.shape[0]
    left = grads.reshape(count, BLOCKS, width_out).astype(jnp.float32)
    right = weights.reshape(BLOCKS, width_in, width_out).astype(jnp.float32)
    return jnp.einsum('nbc,bkc->nbk', left, right).reshape(count, BLOCKS * width_in)

def outer_sum(values, grads, width_in, width_out):
    count = values.shape[0]
    left = values.reshape(count, BLOCKS, width_in).astype(jnp.float32)
    right = grads.reshape(count, BLOCKS, width_out).astype(jnp.float32)
    return jnp.einsum('nbk,nbc->bkc', left, right).reshape(BLOCKS * width_in, width_out)

def gelu_tanh(values):
    return jax.nn.gelu(values, approximate=True)

def reference(tokens_in, out_grad, left_up, right_up, left_down, right_down):
    first = blockdot(tokens_in, left_up, BLK, BLK).astype(jnp.bfloat16)
    mixed_up = permute(first)
    pre = blockdot(mixed_up, right_up, BLK, FBLK)
    hidden = gelu_tanh(pre).astype(jnp.bfloat16)
    third = blockdot(hidden, left_down, FBLK, BLK).astype(jnp.bfloat16)
    mixed_down = permute(third)
    layer_out = blockdot(mixed_down, right_down, BLK, BLK).astype(jnp.bfloat16)
    grad_right_down = outer_sum(mixed_down, out_grad, BLK, BLK).astype(jnp.bfloat16)
    back_mixed_down = blockdot_t(out_grad, right_down, BLK, BLK).astype(jnp.bfloat16)
    back_third = permute(back_mixed_down)
    grad_left_down = outer_sum(hidden, back_third, FBLK, BLK).astype(jnp.bfloat16)
    back_hidden = blockdot_t(back_third, left_down, FBLK, BLK)
    back_pre = jax.vjp(gelu_tanh, pre)[1](back_hidden)[0].astype(jnp.bfloat16)
    grad_right_up = outer_sum(mixed_up, back_pre, BLK, FBLK).astype(jnp.bfloat16)
    back_mixed_up = blockdot_t(back_pre, right_up, BLK, FBLK).astype(jnp.bfloat16)
    back_first = permute(back_mixed_up)
    grad_left_up = outer_sum(tokens_in, back_first, BLK, BLK).astype(jnp.bfloat16)
    input_grad = blockdot_t(back_first, left_up, BLK, BLK).astype(jnp.bfloat16)
    return (layer_out, input_grad, grad_left_up, grad_right_up, grad_left_down, grad_right_down)
```

```python
import jax
import jax.numpy as jnp
from jax import lax
from jax.experimental import pallas as pl
from jax.experimental.pallas import tpu as pltpu
from jax.sharding import PartitionSpec as P

F32 = jnp.float32
BF16 = jnp.bfloat16
GELU_C = 0.7978845608028654
GELU_A = 0.044715
NT = (((1,), (1,)), ((), ()))
NN = (((1,), (0,)), ((), ()))
TN = (((0,), (0,)), ((), ()))
PARAMS = pltpu.CompilerParams(vmem_limit_bytes=40 * 1024 * 1024)


def dot(left, right, dims=NN):
    return lax.dot_general(left, right, dims, preferred_element_type=F32)


def weave(upper, lower):
    tok = upper.shape[1]
    both = jnp.concatenate([upper.reshape(-1, 8, tok), lower.reshape(-1, 8, tok)], axis=1)
    return both.astype(BF16)


def unweave(both):
    tok = both.shape[2]
    wide = both.astype(F32)
    upper = wide[:, :8].reshape(-1, tok).astype(BF16)
    lower = wide[:, 8:].reshape(-1, tok).astype(BF16)
    return upper, lower


def entry_kernel(tok_ref, grad_ref, left_up_ref, right_down_ref, send_ref):
    left_up_t = left_up_ref[...].astype(F32).T.astype(BF16)
    first = dot(left_up_t, tok_ref[...], NT)
    back = dot(right_down_ref[...], grad_ref[...], NT)
    send_ref[...] = weave(first, back)


def middle_kernel(recv_ref, right_up_ref, right_up_t_ref, left_down_ref, left_down_t_ref,
                  send_ref, hidden_ref, back_pre_ref, mixed_ref, back_third_ref):
    mixed, back_third = unweave(recv_ref[...])
    mixed_ref[...] = mixed
    back_third_ref[...] = back_third
    pre = dot(right_up_t_ref[...], mixed)
    back_hidden = dot(left_down_ref[...], back_third)
    square = pre * pre
    tanh = jnp.tanh(GELU_C * (pre + GELU_A * (pre * square)))
    cdf = 0.5 * (1.0 + tanh)
    hidden = (pre * cdf).astype(BF16)
    slope = cdf + (0.5 * pre) * (1.0 - tanh * tanh) * (GELU_C * (1.0 + (3.0 * GELU_A) * square))
    back_pre = (back_hidden * slope).astype(BF16)
    hidden_ref[...] = hidden
    back_pre_ref[...] = back_pre
    third = dot(left_down_t_ref[...], hidden)
    back_mixed = dot(right_up_ref[...], back_pre)
    send_ref[...] = weave(third, back_mixed)


def middle_grads_kernel(hidden_ref, back_pre_ref, mixed_ref, back_third_ref, out_ref):
    out_ref[0, :256] = dot(hidden_ref[...], back_third_ref[...], NT).astype(BF16)
    out_ref[0, 256:] = dot(mixed_ref[...], back_pre_ref[...], NT).astype(BF16)


def exit_grads_kernel(recv_ref, tok_ref, grad_ref, out_ref, mixed_ref, back_first_ref):
    mixed, back_first = unweave(recv_ref[...])
    mixed_ref[...] = mixed
    back_first_ref[...] = back_first
    out_ref[:256] = dot(mixed, grad_ref[...]).astype(BF16)
    out_ref[256:] = dot(back_first, tok_ref[...]).T.astype(BF16)


def exit_kernel(mixed_ref, back_first_ref, left_up_ref, right_down_ref, out_ref, in_grad_ref):
    left_up_t = left_up_ref[...].astype(F32).T.astype(BF16)
    out_ref[...] = dot(mixed_ref[...], right_down_ref[...], TN).astype(BF16)
    in_grad_ref[...] = dot(back_first_ref[...], left_up_t, TN).astype(BF16)


def shape(dims, dtype=BF16):
    return jax.ShapeDtypeStruct(dims, dtype)


def shift_pairs(inner, step):
    pairs = []
    for z_lo in range(4):
        for y in range(4):
            to = (z_lo * 4 + (y + step) % 4) if inner else (((z_lo + step) % 4) * 4 + y)
            pairs.append((z_lo * 4 + y, to))
    return pairs


def scatter_sum(parts, place, inner):
    total = lax.dynamic_index_in_dim(parts, place, 0, keepdims=False).astype(F32)
    got = []
    for step in (2, 1, 3):
        chunk = lax.dynamic_index_in_dim(parts, (place + step) % 4, 0, keepdims=False)
        got.append(lax.ppermute(chunk, "dp", shift_pairs(inner, step)))
    for piece in got:
        total = total + piece.astype(F32)
    return total.astype(BF16)


def gather_parts(part, place, inner):
    got = [(step, lax.ppermute(part, "dp", shift_pairs(inner, step))) for step in (2, 1, 3)]
    whole = jnp.zeros((4,) + part.shape, part.dtype)
    whole = lax.dynamic_update_index_in_dim(whole, part, place, 0)
    for step, piece in got:
        whole = lax.dynamic_update_index_in_dim(whole, piece, (place + 4 - step) % 4, 0)
    return whole


def exchange(parts, axis):
    return lax.all_to_all(parts, axis, split_axis=0, concat_axis=0, tiled=True)


def on_device(tokens_in, out_grad, left_up, right_up, left_down, right_down):
    tok = tokens_in.shape[0]
    tile = 256
    dp_index = lax.axis_index("dp")
    y, z_lo = dp_index % 4, dp_index // 4

    send = pl.pallas_call(entry_kernel, out_shape=shape((32, 16, tok)), compiler_params=PARAMS)(
        tokens_in, out_grad, left_up, right_down)
    recv = exchange(send, "tensor")

    weight = lambda rows, cols: pl.BlockSpec((rows, cols), lambda i: (0, 0))
    column = lambda rows: pl.BlockSpec((rows, tile), lambda i: (0, i))
    woven = pl.BlockSpec((32, 16, tile), lambda i: (0, 0, i))
    send, hidden, back_pre, mixed_up, back_third = pl.pallas_call(
        middle_kernel,
        grid=(tok // tile,),
        in_specs=[woven, weight(256, 1024), weight(1024, 256), weight(1024, 256), weight(256, 1024)],
        out_specs=[woven, column(1024), column(1024), column(256), column(256)],
        out_shape=[shape((32, 16, tok)), shape((1024, tok)), shape((1024, tok)),
                   shape((256, tok)), shape((256, tok))],
        compiler_params=PARAMS,
    )(recv, right_up, right_up.T, left_down, left_down.T)
    recv = exchange(send, "tensor")

    parts = pl.pallas_call(
        middle_grads_kernel,
        grid=(4,),
        in_specs=[pl.BlockSpec((256, tok), lambda i: (i, 0)), pl.BlockSpec((256, tok), lambda i: (i, 0)),
                  weight(256, tok), weight(256, tok)],
        out_specs=pl.BlockSpec((1, 512, 256), lambda i: (i, 0, 0)),
        out_shape=shape((4, 512, 256)),
        compiler_params=PARAMS,
    )(hidden, back_pre, mixed_up, back_third)
    part = scatter_sum(parts, y, True)
    part = scatter_sum(part.reshape(4, 128, 256), z_lo, False)
    part = gather_parts(part, z_lo, False).reshape(512, 256)
    whole = gather_parts(part, y, True)
    grad_left_down = whole[:, :256].reshape(1024, 256)
    grad_right_up = whole[:, 256:].transpose(1, 0, 2).reshape(256, 1024)

    late, mixed_down, back_first = pl.pallas_call(
        exit_grads_kernel,
        out_shape=[shape((512, 256)), shape((256, tok)), shape((256, tok))],
        compiler_params=PARAMS,
    )(recv, tokens_in, out_grad)
    late = exchange(late.reshape(16, 32, 256), "dp")
    late = jnp.sum(late.astype(F32), axis=0).astype(BF16)
    late = exchange(jnp.broadcast_to(late[None], (16, 32, 256)), "dp").reshape(512, 256)

    layer_out, input_grad = pl.pallas_call(
        exit_kernel,
        out_shape=[shape((tok, 256)), shape((tok, 256))],
        compiler_params=PARAMS,
    )(mixed_down, back_first, left_up, right_down)
    return layer_out, input_grad, late[256:], grad_right_up, grad_left_down, late[:256]


def solution(mesh):
    rows = P("tensor", None)
    return jax.shard_map(
        on_device,
        mesh=mesh,
        in_specs=(P("dp", "tensor"), P("dp", "tensor"), rows, rows, rows, rows),
        out_specs=(P("dp", "tensor"), P("dp", "tensor"), rows, rows, rows, rows),
        check_vma=False,
    )
```

```python
import jax
import jax.numpy as jnp
from jax import lax
from jax.experimental import pallas as pl
from jax.experimental.pallas import tpu as pltpu
from jax.sharding import PartitionSpec as P

F32 = jnp.float32
BF16 = jnp.bfloat16
GELU_C = 0.7978845608028654
GELU_A = 0.044715
NT = (((1,), (1,)), ((), ()))
NN = (((1,), (0,)), ((), ()))
TN = (((0,), (0,)), ((), ()))
PARAMS = pltpu.CompilerParams(vmem_limit_bytes=40 * 1024 * 1024)


def dot(left, right, dims=NN):
    return lax.dot_general(left, right, dims, preferred_element_type=F32)


def weave(upper, lower):
    tok = upper.shape[1]
    both = jnp.concatenate([upper.reshape(-1, 8, tok), lower.reshape(-1, 8, tok)], axis=1)
    return both.astype(BF16)


def unweave(both):
    tok = both.shape[2]
    wide = both.astype(F32)
    upper = wide[:, :8].reshape(-1, tok).astype(BF16)
    lower = wide[:, 8:].reshape(-1, tok).astype(BF16)
    return upper, lower


def entry_kernel(tok_ref, grad_ref, left_up_ref, right_down_ref, send_ref):
    left_up_t = left_up_ref[...].astype(F32).T.astype(BF16)
    first = dot(left_up_t, tok_ref[...], NT)
    back = dot(right_down_ref[...], grad_ref[...], NT)
    send_ref[...] = weave(first, back)


def middle_kernel(recv_ref, right_up_ref, right_up_t_ref, left_down_ref, left_down_t_ref,
                  send_ref, hidden_ref, back_pre_ref, mixed_ref, back_third_ref):
    mixed, back_third = unweave(recv_ref[...])
    mixed_ref[...] = mixed
    back_third_ref[...] = back_third
    pre = dot(right_up_t_ref[...], mixed)
    back_hidden = dot(left_down_ref[...], back_third)
    square = pre * pre
    tanh = jnp.tanh(GELU_C * (pre + GELU_A * (pre * square)))
    cdf = 0.5 * (1.0 + tanh)
    hidden = (pre * cdf).astype(BF16)
    slope = cdf + (0.5 * pre) * (1.0 - tanh * tanh) * (GELU_C * (1.0 + (3.0 * GELU_A) * square))
    back_pre = (back_hidden * slope).astype(BF16)
    hidden_ref[...] = hidden
    back_pre_ref[...] = back_pre
    third = dot(left_down_t_ref[...], hidden)
    back_mixed = dot(right_up_ref[...], back_pre)
    send_ref[...] = weave(third, back_mixed)


def middle_grads_kernel(hidden_ref, back_pre_ref, mixed_ref, back_third_ref, out_ref):
    out_ref[0, :256] = dot(hidden_ref[...], back_third_ref[...], NT).astype(BF16)
    out_ref[0, 256:] = dot(mixed_ref[...], back_pre_ref[...], NT).astype(BF16)


def exit_grads_kernel(recv_ref, tok_ref, grad_ref, out_ref, mixed_ref, back_first_ref):
    mixed, back_first = unweave(recv_ref[...])
    mixed_ref[...] = mixed
    back_first_ref[...] = back_first
    out_ref[:256] = dot(mixed, grad_ref[...]).astype(BF16)
    out_ref[256:] = dot(back_first, tok_ref[...]).T.astype(BF16)


def exit_kernel(mixed_ref, back_first_ref, left_up_ref, right_down_ref, out_ref, in_grad_ref):
    left_up_t = left_up_ref[...].astype(F32).T.astype(BF16)
    out_ref[...] = dot(mixed_ref[...], right_down_ref[...], TN).astype(BF16)
    in_grad_ref[...] = dot(back_first_ref[...], left_up_t, TN).astype(BF16)


def unpack_kernel(place_ref, own_ref, far_ref, near_ref, last_ref, left_down_ref, right_up_ref):
    place = place_ref[0] & 3
    for step, ref in ((0, own_ref), (2, far_ref), (1, near_ref), (3, last_ref)):
        start = pl.multiple_of(((place + 4 - step) & 3) * 256, 256)
        left_down_ref[pl.ds(start, 256), :] = ref[:256]
        right_up_ref[:, pl.ds(start, 256)] = ref[256:]


def hbm(dims):
    return pltpu.HBM(dims, BF16)


def in_hbm(array):
    return pltpu.with_memory_space_constraint(array, pltpu.HBM)


def shift_pairs(inner, step):
    pairs = []
    for z_lo in range(4):
        for y in range(4):
            to = (z_lo * 4 + (y + step) % 4) if inner else (((z_lo + step) % 4) * 4 + y)
            pairs.append((z_lo * 4 + y, to))
    return pairs


def permute(array, inner, step):
    return lax.ppermute(array, "dp", shift_pairs(inner, step))


def four_sum(own, near, far, last):
    return ((own.astype(F32) + far.astype(F32)) + (near.astype(F32) + last.astype(F32))).astype(BF16)


def scatter_sum_y(parts, y):
    chunk = lambda step: lax.dynamic_index_in_dim(parts, (y + step) & 3, 0, keepdims=False)
    far, near, last = (permute(chunk(step), True, step) for step in (2, 1, 3))
    return four_sum(chunk(0), near, far, last)


def all_sum_z(part):
    far, near, last = (permute(part, False, step) for step in (2, 1, 3))
    return four_sum(part, near, far, last)


def exchange(parts, axis):
    return lax.all_to_all(parts, axis, split_axis=0, concat_axis=0, tiled=True)


def on_device(tokens_in, out_grad, left_up, right_up, left_down, right_down):
    tok = tokens_in.shape[0]
    tile = 256
    y = lax.axis_index("dp") & 3

    weight = lambda rows, cols: pl.BlockSpec((rows, cols), lambda i: (0, 0))
    row = pl.BlockSpec((tile, 256), lambda i: (i, 0))
    column = lambda rows: pl.BlockSpec((rows, tile), lambda i: (0, i))
    woven = pl.BlockSpec((32, 16, tile), lambda i: (0, 0, i))
    send = pl.pallas_call(
        entry_kernel,
        grid=(tok // tile,),
        in_specs=[row, row, weight(256, 256), weight(256, 256)],
        out_specs=woven,
        out_shape=hbm((32, 16, tok)),
        compiler_params=PARAMS,
    )(in_hbm(tokens_in), in_hbm(out_grad), in_hbm(left_up), in_hbm(right_down))
    recv = exchange(send, "tensor")

    send, hidden, back_pre, mixed_up, back_third = pl.pallas_call(
        middle_kernel,
        grid=(tok // tile,),
        in_specs=[woven, weight(256, 1024), weight(1024, 256), weight(1024, 256), weight(256, 1024)],
        out_specs=[woven, column(1024), column(1024), column(256), column(256)],
        out_shape=[hbm((32, 16, tok)), hbm((1024, tok)), hbm((1024, tok)),
                   hbm((256, tok)), hbm((256, tok))],
        compiler_params=PARAMS,
    )(recv, right_up, right_up.T, left_down, left_down.T)
    recv = exchange(send, "tensor")

    parts = pl.pallas_call(
        middle_grads_kernel,
        grid=(4,),
        in_specs=[pl.BlockSpec((256, tok), lambda i: (i, 0)), pl.BlockSpec((256, tok), lambda i: (i, 0)),
                  weight(256, tok), weight(256, tok)],
        out_specs=pl.BlockSpec((1, 512, 256), lambda i: (i, 0, 0)),
        out_shape=hbm((4, 512, 256)),
        compiler_params=PARAMS,
    )(in_hbm(hidden), in_hbm(back_pre), in_hbm(mixed_up), in_hbm(back_third))
    part = all_sum_z(scatter_sum_y(parts, y))
    recv, part = lax.optimization_barrier((recv, part))
    pieces = [part] + [permute(part, True, step) for step in (2, 1, 3)]
    late, mixed_down, back_first = pl.pallas_call(
        exit_grads_kernel,
        out_shape=[hbm((512, 256)), hbm((256, tok)), hbm((256, tok))],
        compiler_params=PARAMS,
    )(recv, tokens_in, out_grad)
    late = exchange(late.reshape(16, 32, 256), "dp")
    late, pieces = lax.optimization_barrier((late, pieces))
    late = jnp.sum(late.astype(F32), axis=0).astype(BF16)
    late = exchange(jnp.broadcast_to(late[None], (16, 32, 256)), "dp").reshape(512, 256)

    grad_left_down, grad_right_up = pl.pallas_call(
        unpack_kernel,
        in_specs=[pl.BlockSpec(memory_space=pltpu.SMEM)] + [pl.BlockSpec(memory_space=pltpu.VMEM)] * 4,
        out_shape=[hbm((1024, 256)), hbm((256, 1024))],
        compiler_params=PARAMS,
    )(y.astype(jnp.int32).reshape(1), *pieces)

    layer_out, input_grad = pl.pallas_call(
        exit_kernel,
        grid=(tok // tile,),
        in_specs=[column(256), column(256), weight(256, 256), weight(256, 256)],
        out_specs=[row, row],
        out_shape=[hbm((tok, 256)), hbm((tok, 256))],
        compiler_params=PARAMS,
    )(in_hbm(mixed_down), in_hbm(back_first), in_hbm(left_up), in_hbm(right_down))
    return layer_out, input_grad, late[256:], grad_right_up, grad_left_down, late[:256]


def solution(mesh):
    rows = P("tensor", None)
    return jax.shard_map(
        on_device,
        mesh=mesh,
        in_specs=(P("dp", "tensor"), P("dp", "tensor"), rows, rows, rows, rows),
        out_specs=(P("dp", "tensor"), P("dp", "tensor"), rows, rows, rows, rows),
        check_vma=False,
    )
```

```python
import jax
import jax.numpy as jnp
from jax import lax
from jax.experimental import pallas as pl
from jax.experimental.pallas import tpu as pltpu
from jax.sharding import PartitionSpec as P

F32 = jnp.float32
BF16 = jnp.bfloat16
GELU_C = 0.7978845608028654
GELU_A = 0.044715
NT = (((1,), (1,)), ((), ()))
NN = (((1,), (0,)), ((), ()))
TN = (((0,), (0,)), ((), ()))
PARAMS = pltpu.CompilerParams(vmem_limit_bytes=24 * 1024 * 1024)
ALONG_Y = [[z_lo * 4 + y for y in range(4)] for z_lo in range(4)]
ALONG_Z = [[z_lo * 4 + y for z_lo in range(4)] for y in range(4)]


def dot(left, right, dims=NN):
    return lax.dot_general(left, right, dims, preferred_element_type=F32)


def weave(upper, lower):
    tok = upper.shape[1]
    both = jnp.concatenate([upper.reshape(-1, 8, tok), lower.reshape(-1, 8, tok)], axis=1)
    return both.astype(BF16)


def unweave(both):
    tok = both.shape[2]
    wide = both.astype(F32)
    upper = wide[:, :8].reshape(-1, tok).astype(BF16)
    lower = wide[:, 8:].reshape(-1, tok).astype(BF16)
    return upper, lower


def entry_kernel(tok_ref, grad_ref, left_up_ref, right_down_ref, send_ref):
    left_up_t = left_up_ref[...].astype(F32).T.astype(BF16)
    first = dot(left_up_t, tok_ref[...], NT)
    back = dot(right_down_ref[...], grad_ref[...], NT)
    send_ref[...] = weave(first, back)


def middle_kernel(recv_ref, right_up_ref, right_up_t_ref, left_down_ref, left_down_t_ref,
                  send_ref, hidden_ref, back_pre_ref, mixed_ref, back_third_ref):
    mixed, back_third = unweave(recv_ref[...])
    mixed_ref[...] = mixed
    back_third_ref[...] = back_third
    pre = dot(right_up_t_ref[...], mixed)
    back_hidden = dot(left_down_ref[...], back_third)
    square = pre * pre
    tanh = jnp.tanh(GELU_C * (pre + GELU_A * (pre * square)))
    cdf = 0.5 * (1.0 + tanh)
    hidden = (pre * cdf).astype(BF16)
    slope = cdf + (0.5 * pre) * (1.0 - tanh * tanh) * (GELU_C * (1.0 + (3.0 * GELU_A) * square))
    back_pre = (back_hidden * slope).astype(BF16)
    hidden_ref[...] = hidden
    back_pre_ref[...] = back_pre
    third = dot(left_down_t_ref[...], hidden)
    back_mixed = dot(right_up_ref[...], back_pre)
    send_ref[...] = weave(third, back_mixed)


def middle_grads_kernel(place_ref, hidden_ref, back_pre_ref, mixed_ref, back_third_ref, *out_refs):
    for step, out_ref in enumerate(out_refs):
        start = pl.multiple_of(((place_ref[0] + step) & 3) * 256, 256)
        block = pl.ds(start, 256)
        out_ref[:256] = dot(hidden_ref[block, :], back_third_ref[...], NT).astype(BF16)
        out_ref[256:] = dot(mixed_ref[...], back_pre_ref[block, :], NT).astype(BF16)


def fold_kernel(place_ref, own_ref, near_ref, far_ref, last_ref, *rest):
    total_ref = rest[-1]
    total_ref[...] = four_sum(own_ref[...], near_ref[...], far_ref[...], last_ref[...])
    for step, out_ref in enumerate(rest[:-1]):
        start = pl.multiple_of(((place_ref[0] + step) & 3) * 128, 128)
        out_ref[...] = total_ref[pl.ds(start, 128), :]


def exit_grads_kernel(recv_ref, tok_ref, grad_ref, out_ref, mixed_ref, back_first_ref):
    mixed, back_first = unweave(recv_ref[...])
    mixed_ref[...] = mixed
    back_first_ref[...] = back_first
    out_ref[:256] = dot(mixed, grad_ref[...]).astype(BF16)
    out_ref[256:] = dot(back_first, tok_ref[...]).T.astype(BF16)


def exit_kernel(mixed_ref, back_first_ref, left_up_ref, right_down_ref, out_ref, in_grad_ref):
    left_up_t = left_up_ref[...].astype(F32).T.astype(BF16)
    out_ref[...] = dot(mixed_ref[...], right_down_ref[...], TN).astype(BF16)
    in_grad_ref[...] = dot(back_first_ref[...], left_up_t, TN).astype(BF16)


def sum_spread_kernel(parts_ref, out_ref):
    total = jnp.sum(parts_ref[...].astype(F32), axis=0).astype(BF16)
    out_ref[...] = jnp.broadcast_to(total[None], out_ref.shape)


def pack_kernel(place_ref, late_ref, own_ref, near_ref, far_ref, last_ref, out_ref):
    late = jnp.sum(late_ref[...].astype(F32), axis=0).astype(BF16)
    place = place_ref[0] & 3
    for peer in range(4):
        out_ref[peer, :128] = late
        for step, ref in ((0, own_ref), (1, near_ref), (2, far_ref), (3, last_ref)):
            start = pl.multiple_of(128 + ((place + 4 - step) & 3) * 128, 128)
            out_ref[peer, pl.ds(start, 128), :] = ref[...]


def unpack_kernel(all_ref, left_up_ref, right_up_ref, left_down_ref, right_down_ref):
    for y in range(4):
        late_ref = right_down_ref if y < 2 else left_up_ref
        late_ref[y % 2 * 128:y % 2 * 128 + 128] = all_ref[y, :128]
        left_down_ref[y * 256:y * 256 + 256] = all_ref[y, 128:384]
        right_up_ref[:, y * 256:y * 256 + 256] = all_ref[y, 384:]


def hbm(dims):
    return pltpu.HBM(dims, BF16)


def plain(dims):
    return jax.ShapeDtypeStruct(dims, BF16)


def in_hbm(array):
    return pltpu.with_memory_space_constraint(array, pltpu.HBM)


def shift_pairs(inner, step):
    pairs = []
    for z_lo in range(4):
        for y in range(4):
            to = (z_lo * 4 + (y + step) % 4) if inner else (((z_lo + step) % 4) * 4 + y)
            pairs.append((z_lo * 4 + y, to))
    return pairs


def permute(array, inner, step):
    return lax.ppermute(array, "dp", shift_pairs(inner, step))


def four_sum(own, near, far, last):
    return ((own.astype(F32) + far.astype(F32)) + (near.astype(F32) + last.astype(F32))).astype(BF16)


def send_on(chunks, inner):
    far = permute(chunks[2], inner, 2)
    near = permute(chunks[1], inner, 1)
    return [chunks[0], near, far, permute(chunks[3], inner, 3)]


def exchange(parts, axis, groups=None):
    return lax.all_to_all(parts, axis, 0, 0, axis_index_groups=groups, tiled=True)


def whole_call(kernel, outs, *args):
    return pl.pallas_call(kernel, out_shape=outs, compiler_params=PARAMS)(*args)


def on_device(tokens_in, out_grad, left_up, right_up, left_down, right_down):
    tok = tokens_in.shape[0]
    tile = 256
    dp_index = lax.axis_index("dp")
    y, z_lo = dp_index & 3, dp_index >> 2

    weight = lambda rows, cols: pl.BlockSpec((rows, cols), lambda i: (0, 0))
    column = lambda rows: pl.BlockSpec((rows, tile), lambda i: (0, i))
    woven = lambda cols: pl.BlockSpec((32, 16, cols), lambda i: (0, 0, i))
    half = pl.BlockSpec((tok // 2, 256), lambda i: (i, 0))
    send = pl.pallas_call(
        entry_kernel,
        grid=(2,),
        in_specs=[half, half, weight(256, 256), weight(256, 256)],
        out_specs=woven(tok // 2),
        out_shape=hbm((32, 16, tok)),
        compiler_params=PARAMS,
    )(in_hbm(tokens_in), in_hbm(out_grad), in_hbm(left_up), in_hbm(right_down))
    recv = exchange(send, "tensor")

    send, hidden, back_pre, mixed_up, back_third = pl.pallas_call(
        middle_kernel,
        grid=(tok // tile,),
        in_specs=[woven(tile), weight(256, 1024), weight(1024, 256), weight(1024, 256), weight(256, 1024)],
        out_specs=[woven(tile), column(1024), column(1024), column(256), column(256)],
        out_shape=[hbm((32, 16, tok)), plain((1024, tok)), plain((1024, tok)),
                   plain((256, tok)), plain((256, tok))],
        compiler_params=PARAMS,
    )(recv, right_up, right_up.T, left_down, left_down.T)
    vmem = pl.BlockSpec(memory_space=pltpu.VMEM)
    smem = pl.BlockSpec(memory_space=pltpu.SMEM)
    y_place = y.astype(jnp.int32).reshape(1)
    z_place = z_lo.astype(jnp.int32).reshape(1)
    parts = pl.pallas_call(
        middle_grads_kernel,
        in_specs=[smem] + [vmem] * 4,
        out_shape=[hbm((512, 256))] * 4,
        compiler_params=PARAMS,
    )(y_place, hidden, back_pre, mixed_up, back_third)
    send, parts = lax.optimization_barrier((send, parts))
    recv = exchange(send, "tensor")

    parts = pl.pallas_call(
        fold_kernel,
        in_specs=[smem] + [vmem] * 4,
        out_shape=[plain((128, 256))] * 4,
        scratch_shapes=[pltpu.VMEM((512, 256), BF16)],
        compiler_params=PARAMS,
    )(z_place, *send_on(parts, True))
    part = four_sum(*send_on(parts, False))
    pieces = send_on([part] * 4, False)
    recv, pieces = lax.optimization_barrier((recv, pieces))

    late, mixed_down, back_first = whole_call(
        exit_grads_kernel, [hbm((512, 256)), plain((256, tok)), plain((256, tok))],
        recv, tokens_in, out_grad)
    late = exchange(late.reshape(4, 128, 256), "dp", ALONG_Y)
    late = whole_call(sum_spread_kernel, hbm((4, 128, 256)), late)
    late = exchange(late, "dp", ALONG_Z)
    packed = pl.pallas_call(
        pack_kernel,
        in_specs=[smem] + [vmem] * 5,
        out_shape=hbm((4, 640, 256)),
        compiler_params=PARAMS,
    )(z_place, late, *pieces)
    packed = exchange(packed, "dp", ALONG_Y)
    layer_out, input_grad = whole_call(
        exit_kernel, [hbm((tok, 256)), hbm((tok, 256))], mixed_down, back_first, left_up, right_down)
    grads = whole_call(
        unpack_kernel, [hbm((256, 256)), hbm((256, 1024)), hbm((1024, 256)), hbm((256, 256))], packed)
    return (layer_out, input_grad, *grads)


def solution(mesh):
    rows = P("tensor", None)
    return jax.shard_map(
        on_device,
        mesh=mesh,
        in_specs=(P("dp", "tensor"), P("dp", "tensor"), rows, rows, rows, rows),
        out_specs=(P("dp", "tensor"), P("dp", "tensor"), rows, rows, rows, rows),
        check_vma=False,
    )
```

```python
import jax
import jax.numpy as jnp
from jax import lax
from jax.experimental import pallas as pl
from jax.experimental.pallas import tpu as pltpu
from jax.sharding import PartitionSpec as P

F32 = jnp.float32
BF16 = jnp.bfloat16
GELU_C = 0.7978845608028654
GELU_A = 0.044715
NT = (((1,), (1,)), ((), ()))
NN = (((1,), (0,)), ((), ()))
TN = (((0,), (0,)), ((), ()))
PARAMS = pltpu.CompilerParams(vmem_limit_bytes=24 * 1024 * 1024)
ALONG_Y = [[z_lo * 4 + y for y in range(4)] for z_lo in range(4)]
ALONG_Z = [[z_lo * 4 + y for z_lo in range(4)] for y in range(4)]


def dot(left, right, dims=NN):
    return lax.dot_general(left, right, dims, preferred_element_type=F32)


def weave(upper, lower):
    tok = upper.shape[1]
    both = jnp.concatenate([upper.reshape(-1, 8, tok), lower.reshape(-1, 8, tok)], axis=1)
    return both.astype(BF16)


def unweave(both):
    tok = both.shape[2]
    wide = both.astype(F32)
    upper = wide[:, :8].reshape(-1, tok).astype(BF16)
    lower = wide[:, 8:].reshape(-1, tok).astype(BF16)
    return upper, lower


def entry_kernel(tok_ref, grad_ref, left_up_ref, right_down_ref, send_ref):
    left_up_t = left_up_ref[...].astype(F32).T.astype(BF16)
    first = dot(left_up_t, tok_ref[...], NT)
    back = dot(right_down_ref[...], grad_ref[...], NT)
    send_ref[...] = weave(first, back)


def middle_kernel(recv_ref, right_up_ref, right_up_t_ref, left_down_ref, left_down_t_ref,
                  send_ref, hidden_ref, back_pre_ref, mixed_ref, back_third_ref):
    mixed, back_third = unweave(recv_ref[...])
    mixed_ref[...] = mixed
    back_third_ref[...] = back_third
    pre = dot(right_up_t_ref[...], mixed)
    back_hidden = dot(left_down_ref[...], back_third)
    square = pre * pre
    tanh = jnp.tanh(GELU_C * (pre + GELU_A * (pre * square)))
    cdf = 0.5 * (1.0 + tanh)
    hidden = (pre * cdf).astype(BF16)
    slope = cdf + (0.5 * pre) * (1.0 - tanh * tanh) * (GELU_C * (1.0 + (3.0 * GELU_A) * square))
    back_pre = (back_hidden * slope).astype(BF16)
    hidden_ref[...] = hidden
    back_pre_ref[...] = back_pre
    third = dot(left_down_t_ref[...], hidden)
    back_mixed = dot(right_up_ref[...], back_pre)
    send_ref[...] = weave(third, back_mixed)


def middle_grads_kernel(place_ref, hidden_ref, back_pre_ref, mixed_ref, back_third_ref, *out_refs):
    for step, out_ref in enumerate(out_refs):
        start = pl.multiple_of(((place_ref[0] + step) & 3) * 256, 256)
        block = pl.ds(start, 256)
        out_ref[:256] = dot(hidden_ref[block, :], back_third_ref[...], NT).astype(BF16)
        out_ref[256:] = dot(mixed_ref[...], back_pre_ref[block, :], NT).astype(BF16)


def fold_kernel(place_ref, own_ref, near_ref, far_ref, last_ref, *rest):
    total_ref = rest[-1]
    total_ref[...] = four_sum(own_ref[...], near_ref[...], far_ref[...], last_ref[...])
    for step, out_ref in enumerate(rest[:-1]):
        start = pl.multiple_of(((place_ref[0] + step) & 3) * 128, 128)
        out_ref[...] = total_ref[pl.ds(start, 128), :]


def exit_grads_kernel(recv_ref, tok_ref, grad_ref, out_ref, mixed_ref, back_first_ref):
    mixed, back_first = unweave(recv_ref[...])
    mixed_ref[...] = mixed
    back_first_ref[...] = back_first
    out_ref[:256] = dot(mixed, grad_ref[...]).astype(BF16)
    out_ref[256:] = dot(back_first, tok_ref[...]).T.astype(BF16)


def exit_kernel(mixed_ref, back_first_ref, left_up_ref, right_down_ref, out_ref, in_grad_ref):
    left_up_t = left_up_ref[...].astype(F32).T.astype(BF16)
    out_ref[...] = dot(mixed_ref[...], right_down_ref[...], TN).astype(BF16)
    in_grad_ref[...] = dot(back_first_ref[...], left_up_t, TN).astype(BF16)


def spread_kernel(late_ref, own_ref, near_ref, far_ref, last_ref, out_ref):
    late = jnp.sum(late_ref[...].astype(F32), axis=0).astype(BF16)
    early = four_sum(own_ref[...], near_ref[...], far_ref[...], last_ref[...])
    for peer in range(4):
        out_ref[peer, :128] = late
        out_ref[peer, 128:] = early


def pack_kernel(parts_ref, out_ref):
    late = jnp.sum(parts_ref[:, :128].astype(F32), axis=0).astype(BF16)
    for peer in range(4):
        out_ref[peer, :128] = late
        for z_lo in range(4):
            out_ref[peer, 128 + z_lo * 128:256 + z_lo * 128] = parts_ref[z_lo, 128:]


def unpack_kernel(all_ref, left_up_ref, right_up_ref, left_down_ref, right_down_ref):
    for y in range(4):
        late_ref = right_down_ref if y < 2 else left_up_ref
        late_ref[y % 2 * 128:y % 2 * 128 + 128] = all_ref[y, :128]
        left_down_ref[y * 256:y * 256 + 256] = all_ref[y, 128:384]
        right_up_ref[:, y * 256:y * 256 + 256] = all_ref[y, 384:]


def hbm(dims):
    return pltpu.HBM(dims, BF16)


def plain(dims):
    return jax.ShapeDtypeStruct(dims, BF16)


def in_hbm(array):
    return pltpu.with_memory_space_constraint(array, pltpu.HBM)


def shift_pairs(inner, step):
    pairs = []
    for z_lo in range(4):
        for y in range(4):
            to = (z_lo * 4 + (y + step) % 4) if inner else (((z_lo + step) % 4) * 4 + y)
            pairs.append((z_lo * 4 + y, to))
    return pairs


def permute(array, inner, step):
    return lax.ppermute(array, "dp", shift_pairs(inner, step))


def four_sum(own, near, far, last):
    return ((own.astype(F32) + far.astype(F32)) + (near.astype(F32) + last.astype(F32))).astype(BF16)


def send_on(chunks, inner):
    far = permute(chunks[2], inner, 2)
    near = permute(chunks[1], inner, 1)
    return [chunks[0], near, far, permute(chunks[3], inner, 3)]


def exchange(parts, axis, groups=None):
    return lax.all_to_all(parts, axis, 0, 0, axis_index_groups=groups, tiled=True)


def whole_call(kernel, outs, *args):
    return pl.pallas_call(kernel, out_shape=outs, compiler_params=PARAMS)(*args)


def on_device(tokens_in, out_grad, left_up, right_up, left_down, right_down):
    tok = tokens_in.shape[0]
    tile = 256
    dp_index = lax.axis_index("dp")
    y, z_lo = dp_index & 3, dp_index >> 2

    weight = lambda rows, cols: pl.BlockSpec((rows, cols), lambda i: (0, 0))
    column = lambda rows: pl.BlockSpec((rows, tile), lambda i: (0, i))
    woven = lambda cols: pl.BlockSpec((32, 16, cols), lambda i: (0, 0, i))
    half = pl.BlockSpec((tok // 2, 256), lambda i: (i, 0))
    send = pl.pallas_call(
        entry_kernel,
        grid=(2,),
        in_specs=[half, half, weight(256, 256), weight(256, 256)],
        out_specs=woven(tok // 2),
        out_shape=hbm((32, 16, tok)),
        compiler_params=PARAMS,
    )(in_hbm(tokens_in), in_hbm(out_grad), in_hbm(left_up), in_hbm(right_down))
    recv = exchange(send, "tensor")

    send, hidden, back_pre, mixed_up, back_third = pl.pallas_call(
        middle_kernel,
        grid=(tok // tile,),
        in_specs=[woven(tile), weight(256, 1024), weight(1024, 256), weight(1024, 256), weight(256, 1024)],
        out_specs=[woven(tile), column(1024), column(1024), column(256), column(256)],
        out_shape=[hbm((32, 16, tok)), plain((1024, tok)), plain((1024, tok)),
                   plain((256, tok)), plain((256, tok))],
        compiler_params=PARAMS,
    )(recv, right_up, right_up.T, left_down, left_down.T)
    vmem = pl.BlockSpec(memory_space=pltpu.VMEM)
    smem = pl.BlockSpec(memory_space=pltpu.SMEM)
    y_place = y.astype(jnp.int32).reshape(1)
    z_place = z_lo.astype(jnp.int32).reshape(1)
    parts = pl.pallas_call(
        middle_grads_kernel,
        in_specs=[smem] + [vmem] * 4,
        out_shape=[hbm((512, 256))] * 4,
        compiler_params=PARAMS,
    )(y_place, hidden, back_pre, mixed_up, back_third)
    send, parts = lax.optimization_barrier((send, parts))
    recv = exchange(send, "tensor")

    parts = pl.pallas_call(
        fold_kernel,
        in_specs=[smem] + [vmem] * 4,
        out_shape=[plain((128, 256))] * 4,
        scratch_shapes=[pltpu.VMEM((512, 256), BF16)],
        compiler_params=PARAMS,
    )(z_place, *send_on(parts, True))
    pieces = send_on(parts, False)
    recv, pieces = lax.optimization_barrier((recv, pieces))

    late, mixed_down, back_first = whole_call(
        exit_grads_kernel, [hbm((512, 256)), plain((256, tok)), plain((256, tok))],
        recv, tokens_in, out_grad)
    late = exchange(late.reshape(4, 128, 256), "dp", ALONG_Y)
    late = whole_call(spread_kernel, hbm((4, 256, 256)), late, *pieces)
    late = exchange(late, "dp", ALONG_Z)
    packed = whole_call(pack_kernel, hbm((4, 640, 256)), late)
    packed = exchange(packed, "dp", ALONG_Y)
    layer_out, input_grad = whole_call(
        exit_kernel, [hbm((tok, 256)), hbm((tok, 256))], mixed_down, back_first, left_up, right_down)
    grads = whole_call(
        unpack_kernel, [hbm((256, 256)), hbm((256, 1024)), hbm((1024, 256)), hbm((256, 256))], packed)
    return (layer_out, input_grad, *grads)


def solution(mesh):
    rows = P("tensor", None)
    return jax.shard_map(
        on_device,
        mesh=mesh,
        in_specs=(P("dp", "tensor"), P("dp", "tensor"), rows, rows, rows, rows),
        out_specs=(P("dp", "tensor"), P("dp", "tensor"), rows, rows, rows, rows),
        check_vma=False,
    )
```

```python
import jax
import jax.numpy as jnp
from jax import lax
from jax.experimental import pallas as pl
from jax.experimental.pallas import tpu as pltpu
from jax.sharding import PartitionSpec as P

F32 = jnp.float32
BF16 = jnp.bfloat16
GELU_C = 0.7978845608028654
GELU_A = 0.044715
NT = (((1,), (1,)), ((), ()))
NN = (((1,), (0,)), ((), ()))
TN = (((0,), (0,)), ((), ()))
PARAMS = pltpu.CompilerParams(vmem_limit_bytes=24 * 1024 * 1024)
ALONG_Y = [[z_lo * 4 + y for y in range(4)] for z_lo in range(4)]
ALONG_Z = [[z_lo * 4 + y for z_lo in range(4)] for y in range(4)]


def dot(left, right, dims=NN):
    return lax.dot_general(left, right, dims, preferred_element_type=F32)


def weave(upper, lower):
    tok = upper.shape[1]
    both = jnp.concatenate([upper.reshape(-1, 8, tok), lower.reshape(-1, 8, tok)], axis=1)
    return both.astype(BF16)


def unweave(both):
    tok = both.shape[2]
    wide = both.astype(F32)
    upper = wide[:, :8].reshape(-1, tok).astype(BF16)
    lower = wide[:, 8:].reshape(-1, tok).astype(BF16)
    return upper, lower


def entry_kernel(tok_ref, grad_ref, left_up_ref, right_down_ref, send_ref):
    left_up_t = left_up_ref[...].astype(F32).T.astype(BF16)
    first = dot(left_up_t, tok_ref[...], NT)
    back = dot(right_down_ref[...], grad_ref[...], NT)
    send_ref[...] = weave(first, back)


def middle_kernel(recv_ref, right_up_ref, right_up_t_ref, left_down_ref, left_down_t_ref,
                  send_ref, hidden_ref, back_pre_ref, mixed_ref, back_third_ref):
    mixed, back_third = unweave(recv_ref[...])
    mixed_ref[...] = mixed
    back_third_ref[...] = back_third
    pre = dot(right_up_t_ref[...], mixed)
    back_hidden = dot(left_down_ref[...], back_third)
    square = pre * pre
    tanh = jnp.tanh(GELU_C * (pre + GELU_A * (pre * square)))
    cdf = 0.5 * (1.0 + tanh)
    hidden = (pre * cdf).astype(BF16)
    slope = cdf + (0.5 * pre) * (1.0 - tanh * tanh) * (GELU_C * (1.0 + (3.0 * GELU_A) * square))
    back_pre = (back_hidden * slope).astype(BF16)
    hidden_ref[...] = hidden
    back_pre_ref[...] = back_pre
    third = dot(left_down_t_ref[...], hidden)
    back_mixed = dot(right_up_ref[...], back_pre)
    send_ref[...] = weave(third, back_mixed)


def middle_grads_kernel(place_ref, hidden_hbm, back_pre_hbm, mixed_hbm, back_third_hbm,
                        own_ref, near_ref, far_ref, last_ref,
                        hidden_ref, back_pre_ref, mixed_ref, back_third_ref, sems):
    small = [pltpu.make_async_copy(mixed_hbm, mixed_ref, sems.at[0]),
             pltpu.make_async_copy(back_third_hbm, back_third_ref, sems.at[1])]
    large = []
    for step in range(4):
        rows = pl.ds(pl.multiple_of(((place_ref[0] + step) & 3) * 256, 256), 256)
        large.append((pltpu.make_async_copy(hidden_hbm.at[rows], hidden_ref.at[step], sems.at[2 + step]),
                      pltpu.make_async_copy(back_pre_hbm.at[rows], back_pre_ref.at[step], sems.at[6 + step])))
    for copy in small:
        copy.start()
    for pair in large:
        for copy in pair:
            copy.start()
    for copy in small:
        copy.wait()
    for step, out_ref in enumerate((own_ref, near_ref, far_ref, last_ref)):
        large[step][0].wait()
        out_ref[:256] = dot(hidden_ref[step], back_third_ref[...], NT).astype(BF16)
        large[step][1].wait()
        out_ref[256:] = dot(mixed_ref[...], back_pre_ref[step], NT).astype(BF16)


def fold_kernel(place_ref, own_ref, near_ref, far_ref, last_ref, *rest):
    total_ref = rest[-1]
    total_ref[...] = four_sum(own_ref[...], near_ref[...], far_ref[...], last_ref[...])
    for step, out_ref in enumerate(rest[:-1]):
        start = pl.multiple_of(((place_ref[0] + step) & 3) * 128, 128)
        out_ref[...] = total_ref[pl.ds(start, 128), :]


def exit_grads_kernel(recv_ref, tok_hbm, grad_hbm, out_ref, mixed_ref, back_first_ref,
                      tok_ref, grad_ref, sems):
    grad_copy = pltpu.make_async_copy(grad_hbm, grad_ref, sems.at[0])
    tok_copy = pltpu.make_async_copy(tok_hbm, tok_ref, sems.at[1])
    grad_copy.start()
    tok_copy.start()
    mixed, back_first = unweave(recv_ref[...])
    mixed_ref[...] = mixed
    back_first_ref[...] = back_first
    grad_copy.wait()
    out_ref[:256] = dot(mixed, grad_ref[...]).astype(BF16)
    tok_copy.wait()
    out_ref[256:] = dot(back_first, tok_ref[...]).T.astype(BF16)


def exit_kernel(mixed_ref, back_first_ref, left_up_ref, right_down_ref, out_ref, in_grad_ref):
    left_up_t = left_up_ref[...].astype(F32).T.astype(BF16)
    out_ref[...] = dot(mixed_ref[...], right_down_ref[...], TN).astype(BF16)
    in_grad_ref[...] = dot(back_first_ref[...], left_up_t, TN).astype(BF16)


def spread_kernel(late_ref, own_ref, near_ref, far_ref, last_ref, out_ref):
    late = jnp.sum(late_ref[...].astype(F32), axis=0).astype(BF16)
    early = four_sum(own_ref[...], near_ref[...], far_ref[...], last_ref[...])
    for peer in range(4):
        out_ref[peer, :32] = late
        out_ref[peer, 32:] = early


def pack_kernel(parts_ref, out_ref):
    for peer in range(4):
        for z_lo in range(4):
            out_ref[peer, z_lo * 32:z_lo * 32 + 32] = parts_ref[z_lo, :32]
            out_ref[peer, 128 + z_lo * 128:256 + z_lo * 128] = parts_ref[z_lo, 32:]


def unpack_kernel(all_ref, left_up_ref, right_up_ref, left_down_ref, right_down_ref):
    for y in range(4):
        for z_lo in range(4):
            start = (z_lo * 4 + y) * 32
            late_ref = right_down_ref if start < 256 else left_up_ref
            late_ref[start % 256:start % 256 + 32] = all_ref[y, z_lo * 32:z_lo * 32 + 32]
        left_down_ref[y * 256:y * 256 + 256] = all_ref[y, 128:384]
        right_up_ref[:, y * 256:y * 256 + 256] = all_ref[y, 384:]


def hbm(dims):
    return pltpu.HBM(dims, BF16)


def plain(dims):
    return jax.ShapeDtypeStruct(dims, BF16)


def in_hbm(array):
    return pltpu.with_memory_space_constraint(array, pltpu.HBM)


def shift_pairs(inner, step):
    pairs = []
    for z_lo in range(4):
        for y in range(4):
            to = (z_lo * 4 + (y + step) % 4) if inner else (((z_lo + step) % 4) * 4 + y)
            pairs.append((z_lo * 4 + y, to))
    return pairs


def permute(array, inner, step):
    return lax.ppermute(array, "dp", shift_pairs(inner, step))


def four_sum(own, near, far, last):
    return ((own.astype(F32) + far.astype(F32)) + (near.astype(F32) + last.astype(F32))).astype(BF16)


def send_on(chunks, inner):
    far = permute(chunks[2], inner, 2)
    near = permute(chunks[1], inner, 1)
    return [chunks[0], near, far, permute(chunks[3], inner, 3)]


def exchange(parts, axis, groups=None):
    return lax.all_to_all(parts, axis, 0, 0, axis_index_groups=groups, tiled=True)


def whole_call(kernel, outs, *args):
    return pl.pallas_call(kernel, out_shape=outs, compiler_params=PARAMS)(*args)


def on_device(tokens_in, out_grad, left_up, right_up, left_down, right_down):
    tok = tokens_in.shape[0]
    tile = 256
    dp_index = lax.axis_index("dp")
    y, z_lo = dp_index & 3, dp_index >> 2

    weight = lambda rows, cols: pl.BlockSpec((rows, cols), lambda i: (0, 0))
    column = lambda rows: pl.BlockSpec((rows, tile), lambda i: (0, i))
    woven = lambda cols: pl.BlockSpec((32, 16, cols), lambda i: (0, 0, i))
    half = pl.BlockSpec((tok // 2, 256), lambda i: (i, 0))
    send = pl.pallas_call(
        entry_kernel,
        grid=(2,),
        in_specs=[half, half, weight(256, 256), weight(256, 256)],
        out_specs=woven(tok // 2),
        out_shape=hbm((32, 16, tok)),
        compiler_params=PARAMS,
    )(in_hbm(tokens_in), in_hbm(out_grad), in_hbm(left_up), in_hbm(right_down))
    recv = exchange(send, "tensor")

    send, hidden, back_pre, mixed_up, back_third = pl.pallas_call(
        middle_kernel,
        grid=(tok // tile,),
        in_specs=[woven(tile), weight(256, 1024), weight(1024, 256), weight(1024, 256), weight(256, 1024)],
        out_specs=[woven(tile), column(1024), column(1024), column(256), column(256)],
        out_shape=[hbm((32, 16, tok)), hbm((1024, tok)), hbm((1024, tok)),
                   hbm((256, tok)), hbm((256, tok))],
        compiler_params=PARAMS,
    )(recv, right_up, right_up.T, left_down, left_down.T)
    recv = exchange(send, "tensor")

    vmem = pl.BlockSpec(memory_space=pltpu.VMEM)
    smem = pl.BlockSpec(memory_space=pltpu.SMEM)
    far_away = pl.BlockSpec(memory_space=pltpu.HBM)
    y_place = y.astype(jnp.int32).reshape(1)
    z_place = z_lo.astype(jnp.int32).reshape(1)
    parts = pl.pallas_call(
        middle_grads_kernel,
        in_specs=[smem] + [far_away] * 4,
        out_shape=[plain((512, 256))] * 4,
        scratch_shapes=[pltpu.VMEM((4, 256, tok), BF16), pltpu.VMEM((4, 256, tok), BF16),
                        pltpu.VMEM((256, tok), BF16), pltpu.VMEM((256, tok), BF16),
                        pltpu.SemaphoreType.DMA((10,))],
        compiler_params=PARAMS,
    )(y_place, in_hbm(hidden), in_hbm(back_pre), in_hbm(mixed_up), in_hbm(back_third))

    parts = pl.pallas_call(
        fold_kernel,
        in_specs=[smem] + [vmem] * 4,
        out_shape=[plain((128, 256))] * 4,
        scratch_shapes=[pltpu.VMEM((512, 256), BF16)],
        compiler_params=PARAMS,
    )(z_place, *send_on(parts, True))
    pieces = send_on(parts, False)
    recv, pieces = lax.optimization_barrier((recv, pieces))

    late, mixed_down, back_first = pl.pallas_call(
        exit_grads_kernel,
        in_specs=[vmem, far_away, far_away],
        out_shape=[hbm((512, 256)), plain((256, tok)), plain((256, tok))],
        scratch_shapes=[pltpu.VMEM((tok, 256), BF16), pltpu.VMEM((tok, 256), BF16),
                        pltpu.SemaphoreType.DMA((2,))],
        compiler_params=PARAMS,
    )(recv, in_hbm(tokens_in), in_hbm(out_grad))
    late = exchange(late.reshape(16, 32, 256), "dp")
    late = whole_call(spread_kernel, hbm((4, 160, 256)), late, *pieces)
    late = exchange(late, "dp", ALONG_Z)
    packed = whole_call(pack_kernel, hbm((4, 640, 256)), late)
    packed = exchange(packed, "dp", ALONG_Y)
    layer_out, input_grad = whole_call(
        exit_kernel, [hbm((tok, 256)), hbm((tok, 256))], mixed_down, back_first, left_up, right_down)
    grads = whole_call(
        unpack_kernel, [hbm((256, 256)), hbm((256, 1024)), hbm((1024, 256)), hbm((256, 256))], packed)
    return (layer_out, input_grad, *grads)


def solution(mesh):
    rows = P("tensor", None)
    return jax.shard_map(
        on_device,
        mesh=mesh,
        in_specs=(P("dp", "tensor"), P("dp", "tensor"), rows, rows, rows, rows),
        out_specs=(P("dp", "tensor"), P("dp", "tensor"), rows, rows, rows, rows),
        check_vma=False,
    )
```

```python
import jax
import jax.numpy as jnp
from jax import lax
from jax.experimental import pallas as pl
from jax.experimental.pallas import tpu as pltpu
from jax.sharding import PartitionSpec as P

F32 = jnp.float32
BF16 = jnp.bfloat16
GELU_C = 0.7978845608028654
GELU_A = 0.044715
NT = (((1,), (1,)), ((), ()))
NN = (((1,), (0,)), ((), ()))
TN = (((0,), (0,)), ((), ()))
PARAMS = pltpu.CompilerParams(vmem_limit_bytes=24 * 1024 * 1024)


def dot(left, right, dims=NN):
    return lax.dot_general(left, right, dims, preferred_element_type=F32)


def weave(upper, lower):
    tok = upper.shape[1]
    both = jnp.concatenate([upper.reshape(-1, 8, tok), lower.reshape(-1, 8, tok)], axis=1)
    return both.astype(BF16)


def unweave(both):
    tok = both.shape[2]
    wide = both.astype(F32)
    upper = wide[:, :8].reshape(-1, tok).astype(BF16)
    lower = wide[:, 8:].reshape(-1, tok).astype(BF16)
    return upper, lower


def entry_kernel(tok_ref, grad_ref, left_up_ref, right_down_ref, send_ref):
    left_up_t = left_up_ref[...].astype(F32).T.astype(BF16)
    first = dot(left_up_t, tok_ref[...], NT)
    back = dot(right_down_ref[...], grad_ref[...], NT)
    send_ref[...] = weave(first, back)


def middle_kernel(recv_ref, right_up_ref, right_up_t_ref, left_down_ref, left_down_t_ref,
                  send_ref, hidden_ref, back_pre_ref, mixed_ref, back_third_ref):
    mixed, back_third = unweave(recv_ref[...])
    mixed_ref[...] = mixed
    back_third_ref[...] = back_third
    pre = dot(right_up_t_ref[...], mixed)
    back_hidden = dot(left_down_ref[...], back_third)
    square = pre * pre
    tanh = jnp.tanh(GELU_C * (pre + GELU_A * (pre * square)))
    cdf = 0.5 * (1.0 + tanh)
    hidden = (pre * cdf).astype(BF16)
    slope = cdf + (0.5 * pre) * (1.0 - tanh * tanh) * (GELU_C * (1.0 + (3.0 * GELU_A) * square))
    back_pre = (back_hidden * slope).astype(BF16)
    hidden_ref[...] = hidden
    back_pre_ref[...] = back_pre
    third = dot(left_down_t_ref[...], hidden)
    back_mixed = dot(right_up_ref[...], back_pre)
    send_ref[...] = weave(third, back_mixed)


def middle_grads_kernel(place_ref, hidden_hbm, back_pre_hbm, mixed_hbm, back_third_hbm,
                        own_ref, near_ref, far_ref, last_ref,
                        hidden_ref, back_pre_ref, mixed_ref, back_third_ref, sems):
    small = [pltpu.make_async_copy(mixed_hbm, mixed_ref, sems.at[0]),
             pltpu.make_async_copy(back_third_hbm, back_third_ref, sems.at[1])]
    large = []
    for step in range(4):
        rows = pl.ds(pl.multiple_of(((place_ref[0] + step) & 3) * 256, 256), 256)
        large.append((pltpu.make_async_copy(hidden_hbm.at[rows], hidden_ref.at[step], sems.at[2 + step]),
                      pltpu.make_async_copy(back_pre_hbm.at[rows], back_pre_ref.at[step], sems.at[6 + step])))
    for copy in small:
        copy.start()
    for pair in large:
        for copy in pair:
            copy.start()
    for copy in small:
        copy.wait()
    for step, out_ref in enumerate((own_ref, near_ref, far_ref, last_ref)):
        large[step][0].wait()
        out_ref[:256] = dot(hidden_ref[step], back_third_ref[...], NT).astype(BF16)
        large[step][1].wait()
        out_ref[256:] = dot(mixed_ref[...], back_pre_ref[step], NT).astype(BF16)


def fold_kernel(place_ref, own_ref, near_ref, far_ref, last_ref, *rest):
    total_ref = rest[-1]
    total_ref[...] = four_sum(own_ref[...], near_ref[...], far_ref[...], last_ref[...])
    for step, out_ref in enumerate(rest[:-1]):
        start = pl.multiple_of(((place_ref[0] + step) & 3) * 128, 128)
        out_ref[...] = total_ref[pl.ds(start, 128), :]


def exit_grads_kernel(recv_ref, tok_ref, grad_ref, out_ref, mixed_ref, back_first_ref):
    mixed, back_first = unweave(recv_ref[...])
    mixed_ref[...] = mixed
    back_first_ref[...] = back_first
    out_ref[:256] = dot(mixed, grad_ref[...]).astype(BF16)
    out_ref[256:] = dot(back_first, tok_ref[...]).T.astype(BF16)


def exit_kernel(mixed_ref, back_first_ref, left_up_ref, right_down_ref, out_ref, in_grad_ref):
    left_up_t = left_up_ref[...].astype(F32).T.astype(BF16)
    out_ref[...] = dot(mixed_ref[...], right_down_ref[...], TN).astype(BF16)
    in_grad_ref[...] = dot(back_first_ref[...], left_up_t, TN).astype(BF16)


def spread_kernel(place_ref, late_ref, own_ref, near_ref, far_ref, last_ref, late_out_ref, early_out_ref):
    late = jnp.sum(late_ref[...].astype(F32), axis=0).astype(BF16)
    late_out_ref[...] = jnp.broadcast_to(late[None], late_out_ref.shape)
    for step, ref in enumerate((own_ref, near_ref, far_ref, last_ref)):
        start = pl.multiple_of(((place_ref[0] + 4 - step) & 3) * 128, 128)
        early_out_ref[pl.ds(start, 128), :] = ref[...]


def unpack_kernel(place_ref, late_ref, own_ref, near_ref, far_ref, last_ref,
                  left_up_ref, right_up_ref, left_down_ref, right_down_ref):
    right_down_ref[...] = late_ref[:8].reshape(256, 256)
    left_up_ref[...] = late_ref[8:].reshape(256, 256)
    for step, ref in enumerate((own_ref, near_ref, far_ref, last_ref)):
        start = pl.multiple_of(((place_ref[0] + 4 - step) & 3) * 256, 256)
        left_down_ref[pl.ds(start, 256), :] = ref[:256]
        right_up_ref[:, pl.ds(start, 256)] = ref[256:]


def hbm(dims):
    return pltpu.HBM(dims, BF16)


def plain(dims):
    return jax.ShapeDtypeStruct(dims, BF16)


def in_hbm(array):
    return pltpu.with_memory_space_constraint(array, pltpu.HBM)


def shift_pairs(inner, step):
    pairs = []
    for z_lo in range(4):
        for y in range(4):
            to = (z_lo * 4 + (y + step) % 4) if inner else (((z_lo + step) % 4) * 4 + y)
            pairs.append((z_lo * 4 + y, to))
    return pairs


def permute(array, inner, step):
    return lax.ppermute(array, "dp", shift_pairs(inner, step))


def four_sum(own, near, far, last):
    return ((own.astype(F32) + far.astype(F32)) + (near.astype(F32) + last.astype(F32))).astype(BF16)


def send_on(chunks, inner):
    far = permute(chunks[2], inner, 2)
    near = permute(chunks[1], inner, 1)
    return [chunks[0], near, far, permute(chunks[3], inner, 3)]


def exchange(parts, axis):
    return lax.all_to_all(parts, axis, 0, 0, tiled=True)


def whole_call(kernel, outs, *args):
    return pl.pallas_call(kernel, out_shape=outs, compiler_params=PARAMS)(*args)


def on_device(tokens_in, out_grad, left_up, right_up, left_down, right_down):
    tok = tokens_in.shape[0]
    tile = 256
    dp_index = lax.axis_index("dp")
    y, z_lo = dp_index & 3, dp_index >> 2

    weight = lambda rows, cols: pl.BlockSpec((rows, cols), lambda i: (0, 0))
    column = lambda rows: pl.BlockSpec((rows, tile), lambda i: (0, i))
    woven = lambda cols: pl.BlockSpec((32, 16, cols), lambda i: (0, 0, i))
    half = pl.BlockSpec((tok // 2, 256), lambda i: (i, 0))
    send = pl.pallas_call(
        entry_kernel,
        grid=(2,),
        in_specs=[half, half, weight(256, 256), weight(256, 256)],
        out_specs=woven(tok // 2),
        out_shape=hbm((32, 16, tok)),
        compiler_params=PARAMS,
    )(in_hbm(tokens_in), in_hbm(out_grad), in_hbm(left_up), in_hbm(right_down))
    recv = exchange(send, "tensor")

    send, hidden, back_pre, mixed_up, back_third = pl.pallas_call(
        middle_kernel,
        grid=(tok // tile,),
        in_specs=[woven(tile), weight(256, 1024), weight(1024, 256), weight(1024, 256), weight(256, 1024)],
        out_specs=[woven(tile), column(1024), column(1024), column(256), column(256)],
        out_shape=[hbm((32, 16, tok)), hbm((1024, tok)), hbm((1024, tok)),
                   hbm((256, tok)), hbm((256, tok))],
        compiler_params=PARAMS,
    )(recv, right_up, right_up.T, left_down, left_down.T)
    recv = exchange(send, "tensor")

    vmem = pl.BlockSpec(memory_space=pltpu.VMEM)
    smem = pl.BlockSpec(memory_space=pltpu.SMEM)
    far_away = pl.BlockSpec(memory_space=pltpu.HBM)
    y_place = y.astype(jnp.int32).reshape(1)
    z_place = z_lo.astype(jnp.int32).reshape(1)
    parts = pl.pallas_call(
        middle_grads_kernel,
        in_specs=[smem] + [far_away] * 4,
        out_shape=[plain((512, 256))] * 4,
        scratch_shapes=[pltpu.VMEM((4, 256, tok), BF16), pltpu.VMEM((4, 256, tok), BF16),
                        pltpu.VMEM((256, tok), BF16), pltpu.VMEM((256, tok), BF16),
                        pltpu.SemaphoreType.DMA((10,))],
        compiler_params=PARAMS,
    )(y_place, in_hbm(hidden), in_hbm(back_pre), in_hbm(mixed_up), in_hbm(back_third))

    parts = pl.pallas_call(
        fold_kernel,
        in_specs=[smem] + [vmem] * 4,
        out_shape=[plain((128, 256))] * 4,
        scratch_shapes=[pltpu.VMEM((512, 256), BF16)],
        compiler_params=PARAMS,
    )(z_place, *send_on(parts, True))
    pieces = send_on(parts, False)
    part = four_sum(*pieces)
    recv, part = lax.optimization_barrier((recv, part))
    late, mixed_down, back_first = whole_call(
        exit_grads_kernel, [hbm((512, 256)), plain((256, tok)), plain((256, tok))],
        recv, tokens_in, out_grad)

    late = exchange(late.reshape(16, 32, 256), "dp")
    pieces = send_on([part] * 4, False)
    late, part = pl.pallas_call(
        spread_kernel,
        in_specs=[smem] + [vmem] * 5,
        out_shape=[hbm((16, 32, 256)), plain((512, 256))],
        compiler_params=PARAMS,
    )(z_place, late, *pieces)
    late = exchange(late, "dp")
    pieces = send_on([part] * 4, True)
    layer_out, input_grad = whole_call(
        exit_kernel, [hbm((tok, 256)), hbm((tok, 256))], mixed_down, back_first, left_up, right_down)
    grads = pl.pallas_call(
        unpack_kernel,
        in_specs=[smem] + [vmem] * 5,
        out_shape=[hbm((256, 256)), hbm((256, 1024)), hbm((1024, 256)), hbm((256, 256))],
        compiler_params=PARAMS,
    )(y_place, late, *pieces)
    return (layer_out, input_grad, *grads)


def solution(mesh):
    rows = P("tensor", None)
    return jax.shard_map(
        on_device,
        mesh=mesh,
        in_specs=(P("dp", "tensor"), P("dp", "tensor"), rows, rows, rows, rows),
        out_specs=(P("dp", "tensor"), P("dp", "tensor"), rows, rows, rows, rows),
        check_vma=False,
    )
```

```python
import jax
import jax.numpy as jnp
from jax import lax
from jax.experimental import pallas as pl
from jax.experimental.pallas import tpu as pltpu
from jax.sharding import PartitionSpec as P

F32 = jnp.float32
BF16 = jnp.bfloat16
GELU_C = 0.7978845608028654
GELU_A = 0.044715
NT = (((1,), (1,)), ((), ()))
NN = (((1,), (0,)), ((), ()))
TN = (((0,), (0,)), ((), ()))
PARAMS = pltpu.CompilerParams(vmem_limit_bytes=24 * 1024 * 1024)


def dot(left, right, dims=NN):
    return lax.dot_general(left, right, dims, preferred_element_type=F32)


def weave(upper, lower):
    tok = upper.shape[1]
    both = jnp.concatenate([upper.reshape(-1, 8, tok), lower.reshape(-1, 8, tok)], axis=1)
    return both.astype(BF16)


def unweave(both):
    tok = both.shape[2]
    wide = both.astype(F32)
    upper = wide[:, :8].reshape(-1, tok).astype(BF16)
    lower = wide[:, 8:].reshape(-1, tok).astype(BF16)
    return upper, lower


def entry_kernel(tok_ref, grad_ref, left_up_ref, right_down_ref, send_ref):
    left_up_t = left_up_ref[...].astype(F32).T.astype(BF16)
    first = dot(left_up_t, tok_ref[...], NT)
    back = dot(right_down_ref[...], grad_ref[...], NT)
    send_ref[...] = weave(first, back)


def middle_kernel(recv_ref, right_up_ref, right_up_t_ref, left_down_ref, left_down_t_ref,
                  send_ref, hidden_ref, back_pre_ref, mixed_ref, back_third_ref):
    mixed, back_third = unweave(recv_ref[...])
    mixed_ref[...] = mixed
    back_third_ref[...] = back_third
    pre = dot(right_up_t_ref[...], mixed)
    back_hidden = dot(left_down_ref[...], back_third)
    square = pre * pre
    half = 0.5 + 0.5 * jnp.tanh(pre * (GELU_C + (GELU_C * GELU_A) * square))
    hidden = (pre * half).astype(BF16)
    slope = half + (half - half * half) * (pre * (2.0 * GELU_C + (6.0 * GELU_C * GELU_A) * square))
    back_pre = (back_hidden * slope).astype(BF16)
    hidden_ref[...] = hidden
    back_pre_ref[...] = back_pre
    third = dot(left_down_t_ref[...], hidden)
    back_mixed = dot(right_up_ref[...], back_pre)
    send_ref[...] = weave(third, back_mixed)


def middle_grads_kernel(place_ref, hidden_hbm, back_pre_hbm, mixed_hbm, back_third_hbm,
                        own_ref, near_ref, far_ref, last_ref,
                        hidden_ref, back_pre_ref, mixed_ref, back_third_ref, sems):
    small = [pltpu.make_async_copy(mixed_hbm, mixed_ref, sems.at[0]),
             pltpu.make_async_copy(back_third_hbm, back_third_ref, sems.at[1])]
    large = []
    for step in range(4):
        rows = pl.ds(pl.multiple_of(((place_ref[0] + step) & 3) * 256, 256), 256)
        large.append((pltpu.make_async_copy(hidden_hbm.at[rows], hidden_ref.at[step], sems.at[2 + step]),
                      pltpu.make_async_copy(back_pre_hbm.at[rows], back_pre_ref.at[step], sems.at[6 + step])))
    for copy in small:
        copy.start()
    for pair in large:
        for copy in pair:
            copy.start()
    for copy in small:
        copy.wait()
    for step, out_ref in enumerate((own_ref, near_ref, far_ref, last_ref)):
        large[step][0].wait()
        out_ref[:256] = dot(hidden_ref[step], back_third_ref[...], NT).astype(BF16)
        large[step][1].wait()
        out_ref[256:] = dot(mixed_ref[...], back_pre_ref[step], NT).astype(BF16)


def fold_kernel(place_ref, own_ref, near_ref, far_ref, last_ref, keep_ref, give_ref, total_ref):
    total_ref[...] = four_sum(own_ref[...], near_ref[...], far_ref[...], last_ref[...])
    parity = place_ref[0] & 1
    keep_ref[...] = total_ref[pl.ds(pl.multiple_of(parity * 256, 256), 256), :]
    give_ref[...] = total_ref[pl.ds(pl.multiple_of((1 - parity) * 256, 256), 256), :]


def exit_grads_kernel(recv_ref, tok_ref, grad_ref, out_ref, mixed_ref, back_first_ref):
    mixed, back_first = unweave(recv_ref[...])
    mixed_ref[...] = mixed
    back_first_ref[...] = back_first
    out_ref[:256] = dot(mixed, grad_ref[...]).astype(BF16)
    out_ref[256:] = dot(back_first, tok_ref[...]).T.astype(BF16)


def exit_kernel(mixed_ref, back_first_ref, left_up_ref, right_down_ref, out_ref, in_grad_ref):
    left_up_t = left_up_ref[...].astype(F32).T.astype(BF16)
    out_ref[...] = dot(mixed_ref[...], right_down_ref[...], TN).astype(BF16)
    in_grad_ref[...] = dot(back_first_ref[...], left_up_t, TN).astype(BF16)


def spread_kernel(place_ref, late_ref, own_ref, other_ref, late_out_ref, early_out_ref):
    late = jnp.sum(late_ref[...].astype(F32), axis=0).astype(BF16)
    late_out_ref[...] = jnp.broadcast_to(late[None], late_out_ref.shape)
    parity = place_ref[0] & 1
    early_out_ref[pl.ds(pl.multiple_of(parity * 256, 256), 256), :] = own_ref[...]
    early_out_ref[pl.ds(pl.multiple_of((1 - parity) * 256, 256), 256), :] = other_ref[...]


def unpack_kernel(place_ref, late_ref, own_ref, near_ref, far_ref, last_ref,
                  left_up_ref, right_up_ref, left_down_ref, right_down_ref):
    right_down_ref[...] = late_ref[:8].reshape(256, 256)
    left_up_ref[...] = late_ref[8:].reshape(256, 256)
    for step, ref in enumerate((own_ref, near_ref, far_ref, last_ref)):
        start = pl.multiple_of(((place_ref[0] + 4 - step) & 3) * 256, 256)
        left_down_ref[pl.ds(start, 256), :] = ref[:256]
        right_up_ref[:, pl.ds(start, 256)] = ref[256:]


def hbm(dims):
    return pltpu.HBM(dims, BF16)


def plain(dims):
    return jax.ShapeDtypeStruct(dims, BF16)


def in_hbm(array):
    return pltpu.with_memory_space_constraint(array, pltpu.HBM)


def along_y(array, step):
    pairs = [(z_lo * 4 + y, z_lo * 4 + (y + step) % 4) for z_lo in range(4) for y in range(4)]
    return lax.ppermute(array, "dp", pairs)


def swap_z(array, bit):
    pairs = [(z_lo * 4 + y, (z_lo ^ bit) * 4 + y) for z_lo in range(4) for y in range(4)]
    return lax.ppermute(array, "dp", pairs)


def two_sum(own, other):
    return (own.astype(F32) + other.astype(F32)).astype(BF16)


def four_sum(own, near, far, last):
    return ((own.astype(F32) + far.astype(F32)) + (near.astype(F32) + last.astype(F32))).astype(BF16)


def send_on(chunks):
    far = along_y(chunks[2], 2)
    near = along_y(chunks[1], 1)
    return [chunks[0], near, far, along_y(chunks[3], 3)]


def exchange(parts, axis):
    return lax.all_to_all(parts, axis, 0, 0, tiled=True)


def whole_call(kernel, outs, *args):
    return pl.pallas_call(kernel, out_shape=outs, compiler_params=PARAMS)(*args)


def on_device(tokens_in, out_grad, left_up, right_up, left_down, right_down):
    tok = tokens_in.shape[0]
    tile = 256
    dp_index = lax.axis_index("dp")
    y, z_lo = dp_index & 3, dp_index >> 2

    weight = lambda rows, cols: pl.BlockSpec((rows, cols), lambda i: (0, 0))
    column = lambda rows: pl.BlockSpec((rows, tile), lambda i: (0, i))
    woven = lambda cols: pl.BlockSpec((32, 16, cols), lambda i: (0, 0, i))
    half = pl.BlockSpec((tok // 2, 256), lambda i: (i, 0))
    send = pl.pallas_call(
        entry_kernel,
        grid=(2,),
        in_specs=[half, half, weight(256, 256), weight(256, 256)],
        out_specs=woven(tok // 2),
        out_shape=hbm((32, 16, tok)),
        compiler_params=PARAMS,
    )(in_hbm(tokens_in), in_hbm(out_grad), in_hbm(left_up), in_hbm(right_down))
    recv = exchange(send, "tensor")

    send, hidden, back_pre, mixed_up, back_third = pl.pallas_call(
        middle_kernel,
        grid=(tok // tile,),
        in_specs=[woven(tile), weight(256, 1024), weight(1024, 256), weight(1024, 256), weight(256, 1024)],
        out_specs=[woven(tile), column(1024), column(1024), column(256), column(256)],
        out_shape=[hbm((32, 16, tok)), hbm((1024, tok)), hbm((1024, tok)),
                   hbm((256, tok)), hbm((256, tok))],
        compiler_params=PARAMS,
    )(recv, right_up, right_up.T, left_down, left_down.T)
    recv = exchange(send, "tensor")

    vmem = pl.BlockSpec(memory_space=pltpu.VMEM)
    smem = pl.BlockSpec(memory_space=pltpu.SMEM)
    far_away = pl.BlockSpec(memory_space=pltpu.HBM)
    y_place = y.astype(jnp.int32).reshape(1)
    z_place = z_lo.astype(jnp.int32).reshape(1)
    parts = pl.pallas_call(
        middle_grads_kernel,
        in_specs=[smem] + [far_away] * 4,
        out_shape=[plain((512, 256))] * 4,
        scratch_shapes=[pltpu.VMEM((4, 256, tok), BF16), pltpu.VMEM((4, 256, tok), BF16),
                        pltpu.VMEM((256, tok), BF16), pltpu.VMEM((256, tok), BF16),
                        pltpu.SemaphoreType.DMA((10,))],
        compiler_params=PARAMS,
    )(y_place, in_hbm(hidden), in_hbm(back_pre), in_hbm(mixed_up), in_hbm(back_third))

    keep, give = pl.pallas_call(
        fold_kernel,
        in_specs=[smem] + [vmem] * 4,
        out_shape=[plain((256, 256))] * 2,
        scratch_shapes=[pltpu.VMEM((512, 256), BF16)],
        compiler_params=PARAMS,
    )(z_place, *send_on(parts))
    part = two_sum(keep, swap_z(give, 1))
    part = two_sum(part, swap_z(part, 2))
    recv, part = lax.optimization_barrier((recv, part))
    late, mixed_down, back_first = whole_call(
        exit_grads_kernel, [hbm((512, 256)), plain((256, tok)), plain((256, tok))],
        recv, tokens_in, out_grad)

    late = exchange(late.reshape(16, 32, 256), "dp")
    late, part = pl.pallas_call(
        spread_kernel,
        in_specs=[smem] + [vmem] * 3,
        out_shape=[hbm((16, 32, 256)), plain((512, 256))],
        compiler_params=PARAMS,
    )(z_place, late, part, swap_z(part, 1))
    late = exchange(late, "dp")
    pieces = send_on([part] * 4)
    layer_out, input_grad = whole_call(
        exit_kernel, [hbm((tok, 256)), hbm((tok, 256))], mixed_down, back_first, left_up, right_down)
    grads = pl.pallas_call(
        unpack_kernel,
        in_specs=[smem] + [vmem] * 5,
        out_shape=[hbm((256, 256)), hbm((256, 1024)), hbm((1024, 256)), hbm((256, 256))],
        compiler_params=PARAMS,
    )(y_place, late, *pieces)
    return (layer_out, input_grad, *grads)


def solution(mesh):
    rows = P("tensor", None)
    return jax.shard_map(
        on_device,
        mesh=mesh,
        in_specs=(P("dp", "tensor"), P("dp", "tensor"), rows, rows, rows, rows),
        out_specs=(P("dp", "tensor"), P("dp", "tensor"), rows, rows, rows, rows),
        check_vma=False,
    )
```

```python
import jax
import jax.numpy as jnp
from jax import lax
from jax.experimental import pallas as pl
from jax.experimental.pallas import tpu as pltpu
from jax.sharding import PartitionSpec as P

F32 = jnp.float32
BF16 = jnp.bfloat16
GELU_C = 0.7978845608028654
GELU_A = 0.044715
NT = (((1,), (1,)), ((), ()))
NN = (((1,), (0,)), ((), ()))
TN = (((0,), (0,)), ((), ()))
PARAMS = pltpu.CompilerParams(vmem_limit_bytes=24 * 1024 * 1024)


def dot(left, right, dims=NN):
    return lax.dot_general(left, right, dims, preferred_element_type=F32)


def weave(upper, lower):
    tok = upper.shape[1]
    both = jnp.concatenate([upper.reshape(-1, 8, tok), lower.reshape(-1, 8, tok)], axis=1)
    return both.astype(BF16)


def unweave(both):
    tok = both.shape[2]
    wide = both.astype(F32)
    upper = wide[:, :8].reshape(-1, tok).astype(BF16)
    lower = wide[:, 8:].reshape(-1, tok).astype(BF16)
    return upper, lower


def entry_kernel(tok_ref, grad_ref, left_up_ref, right_down_ref, send_ref):
    left_up_t = left_up_ref[...].astype(F32).T.astype(BF16)
    first = dot(left_up_t, tok_ref[...], NT)
    back = dot(right_down_ref[...], grad_ref[...], NT)
    send_ref[...] = weave(first, back)


def middle_kernel(recv_ref, right_up_ref, right_up_t_ref, left_down_ref, left_down_t_ref,
                  send_ref, hidden_ref, back_pre_ref, mixed_ref, back_third_ref):
    mixed, back_third = unweave(recv_ref[...])
    mixed_ref[...] = mixed
    back_third_ref[...] = back_third
    pre = dot(right_up_t_ref[...], mixed)
    back_hidden = dot(left_down_ref[...], back_third)
    square = pre * pre
    half = 0.5 + 0.5 * jnp.tanh(pre * (GELU_C + (GELU_C * GELU_A) * square))
    hidden = (pre * half).astype(BF16)
    slope = half + (half - half * half) * (pre * (2.0 * GELU_C + (6.0 * GELU_C * GELU_A) * square))
    back_pre = (back_hidden * slope).astype(BF16)
    hidden_ref[...] = hidden
    back_pre_ref[...] = back_pre
    third = dot(left_down_t_ref[...], hidden)
    back_mixed = dot(right_up_ref[...], back_pre)
    send_ref[...] = weave(third, back_mixed)


def middle_grads_kernel(place_ref, hidden_hbm, back_pre_hbm, mixed_hbm, back_third_hbm,
                        own_ref, near_ref, far_ref, last_ref,
                        hidden_ref, back_pre_ref, mixed_ref, back_third_ref, sems):
    small = [pltpu.make_async_copy(mixed_hbm, mixed_ref, sems.at[0]),
             pltpu.make_async_copy(back_third_hbm, back_third_ref, sems.at[1])]
    large = []
    for step in range(4):
        rows = pl.ds(pl.multiple_of(((place_ref[0] + step) & 3) * 256, 256), 256)
        large.append((pltpu.make_async_copy(hidden_hbm.at[rows], hidden_ref.at[step], sems.at[2 + step]),
                      pltpu.make_async_copy(back_pre_hbm.at[rows], back_pre_ref.at[step], sems.at[6 + step])))
    for copy in small:
        copy.start()
    for pair in large:
        for copy in pair:
            copy.start()
    for copy in small:
        copy.wait()
    for step, out_ref in enumerate((own_ref, near_ref, far_ref, last_ref)):
        large[step][0].wait()
        out_ref[:256] = dot(hidden_ref[step], back_third_ref[...], NT).astype(BF16)
        large[step][1].wait()
        out_ref[256:] = dot(mixed_ref[...], back_pre_ref[step], NT).astype(BF16)


def exit_grads_kernel(recv_ref, tok_ref, grad_ref, out_ref, mixed_ref, back_first_ref):
    mixed, back_first = unweave(recv_ref[...])
    mixed_ref[...] = mixed
    back_first_ref[...] = back_first
    out_ref[:256] = dot(mixed, grad_ref[...]).astype(BF16)
    out_ref[256:] = dot(back_first, tok_ref[...]).T.astype(BF16)


def exit_kernel(mixed_ref, back_first_ref, left_up_ref, right_down_ref, out_ref, in_grad_ref):
    left_up_t = left_up_ref[...].astype(F32).T.astype(BF16)
    out_ref[...] = dot(mixed_ref[...], right_down_ref[...], TN).astype(BF16)
    in_grad_ref[...] = dot(back_first_ref[...], left_up_t, TN).astype(BF16)


def spread_kernel(late_ref, own_ref, other_ref, late_out_ref, early_out_ref):
    late = jnp.sum(late_ref[...].astype(F32), axis=0).astype(BF16)
    late_out_ref[...] = jnp.broadcast_to(late[None], late_out_ref.shape)
    early_out_ref[...] = two_sum(own_ref[...], other_ref[...])


def unpack_kernel(place_ref, late_ref, own_ref, near_ref, far_ref, last_ref,
                  left_up_ref, right_up_ref, left_down_ref, right_down_ref):
    right_down_ref[...] = late_ref[:8].reshape(256, 256)
    left_up_ref[...] = late_ref[8:].reshape(256, 256)
    for step, ref in enumerate((own_ref, near_ref, far_ref, last_ref)):
        start = pl.multiple_of(((place_ref[0] + 4 - step) & 3) * 256, 256)
        left_down_ref[pl.ds(start, 256), :] = ref[:256]
        right_up_ref[:, pl.ds(start, 256)] = ref[256:]


def hbm(dims):
    return pltpu.HBM(dims, BF16)


def plain(dims):
    return jax.ShapeDtypeStruct(dims, BF16)


def in_hbm(array):
    return pltpu.with_memory_space_constraint(array, pltpu.HBM)


def along_y(array, step):
    pairs = [(z_lo * 4 + y, z_lo * 4 + (y + step) % 4) for z_lo in range(4) for y in range(4)]
    return lax.ppermute(array, "dp", pairs)


def swap_z(array, bit):
    pairs = [(z_lo * 4 + y, (z_lo ^ bit) * 4 + y) for z_lo in range(4) for y in range(4)]
    return lax.ppermute(array, "dp", pairs)


def two_sum(own, other):
    return (own.astype(F32) + other.astype(F32)).astype(BF16)


def four_sum(own, near, far, last):
    return ((own.astype(F32) + far.astype(F32)) + (near.astype(F32) + last.astype(F32))).astype(BF16)


def send_on(chunks):
    far = along_y(chunks[2], 2)
    near = along_y(chunks[1], 1)
    return [chunks[0], near, far, along_y(chunks[3], 3)]


def exchange(parts, axis):
    return lax.all_to_all(parts, axis, 0, 0, tiled=True)


def whole_call(kernel, outs, *args):
    return pl.pallas_call(kernel, out_shape=outs, compiler_params=PARAMS)(*args)


def on_device(tokens_in, out_grad, left_up, right_up, left_down, right_down):
    tok = tokens_in.shape[0]
    tile = 256
    dp_index = lax.axis_index("dp")
    y = dp_index & 3

    weight = lambda rows, cols: pl.BlockSpec((rows, cols), lambda i: (0, 0))
    column = lambda rows: pl.BlockSpec((rows, tile), lambda i: (0, i))
    woven = lambda cols: pl.BlockSpec((32, 16, cols), lambda i: (0, 0, i))
    half = pl.BlockSpec((tok // 2, 256), lambda i: (i, 0))
    send = pl.pallas_call(
        entry_kernel,
        grid=(2,),
        in_specs=[half, half, weight(256, 256), weight(256, 256)],
        out_specs=woven(tok // 2),
        out_shape=hbm((32, 16, tok)),
        compiler_params=PARAMS,
    )(in_hbm(tokens_in), in_hbm(out_grad), in_hbm(left_up), in_hbm(right_down))
    recv = exchange(send, "tensor")

    send, hidden, back_pre, mixed_up, back_third = pl.pallas_call(
        middle_kernel,
        grid=(tok // tile,),
        in_specs=[woven(tile), weight(256, 1024), weight(1024, 256), weight(1024, 256), weight(256, 1024)],
        out_specs=[woven(tile), column(1024), column(1024), column(256), column(256)],
        out_shape=[hbm((32, 16, tok)), hbm((1024, tok)), hbm((1024, tok)),
                   hbm((256, tok)), hbm((256, tok))],
        compiler_params=PARAMS,
    )(recv, right_up, right_up.T, left_down, left_down.T)
    recv = exchange(send, "tensor")

    vmem = pl.BlockSpec(memory_space=pltpu.VMEM)
    smem = pl.BlockSpec(memory_space=pltpu.SMEM)
    far_away = pl.BlockSpec(memory_space=pltpu.HBM)
    y_place = y.astype(jnp.int32).reshape(1)
    parts = pl.pallas_call(
        middle_grads_kernel,
        in_specs=[smem] + [far_away] * 4,
        out_shape=[plain((512, 256))] * 4,
        scratch_shapes=[pltpu.VMEM((4, 256, tok), BF16), pltpu.VMEM((4, 256, tok), BF16),
                        pltpu.VMEM((256, tok), BF16), pltpu.VMEM((256, tok), BF16),
                        pltpu.SemaphoreType.DMA((10,))],
        compiler_params=PARAMS,
    )(y_place, in_hbm(hidden), in_hbm(back_pre), in_hbm(mixed_up), in_hbm(back_third))

    part = four_sum(*send_on(parts))
    part = two_sum(part, swap_z(part, 1))
    recv, part = lax.optimization_barrier((recv, part))
    late, mixed_down, back_first = whole_call(
        exit_grads_kernel, [hbm((512, 256)), hbm((256, tok)), hbm((256, tok))],
        recv, tokens_in, out_grad)

    late = exchange(late.reshape(16, 32, 256), "dp")
    late, part = whole_call(
        spread_kernel, [hbm((16, 32, 256)), plain((512, 256))], late, part, swap_z(part, 2))
    late = exchange(late, "dp")
    pieces = send_on([part] * 4)
    layer_out, input_grad = whole_call(
        exit_kernel, [hbm((tok, 256)), hbm((tok, 256))], mixed_down, back_first, left_up, right_down)
    grads = pl.pallas_call(
        unpack_kernel,
        in_specs=[smem] + [vmem] * 5,
        out_shape=[hbm((256, 256)), hbm((256, 1024)), hbm((1024, 256)), hbm((256, 256))],
        compiler_params=PARAMS,
    )(y_place, late, *pieces)
    return (layer_out, input_grad, *grads)


def solution(mesh):
    rows = P("tensor", None)
    return jax.shard_map(
        on_device,
        mesh=mesh,
        in_specs=(P("dp", "tensor"), P("dp", "tensor"), rows, rows, rows, rows),
        out_specs=(P("dp", "tensor"), P("dp", "tensor"), rows, rows, rows, rows),
        check_vma=False,
    )
```

```python
import jax
import jax.numpy as jnp
from jax import lax
from jax.experimental import pallas as pl
from jax.experimental.pallas import tpu as pltpu
from jax.sharding import PartitionSpec as P

F32 = jnp.float32
BF16 = jnp.bfloat16
GELU_C = 0.7978845608028654
GELU_A = 0.044715
NT = (((1,), (1,)), ((), ()))
NN = (((1,), (0,)), ((), ()))
TN = (((0,), (0,)), ((), ()))
PARAMS = pltpu.CompilerParams(vmem_limit_bytes=24 * 1024 * 1024)


def dot(left, right, dims=NN):
    return lax.dot_general(left, right, dims, preferred_element_type=F32)


def weave(upper, lower):
    tok = upper.shape[1]
    both = jnp.concatenate([upper.reshape(-1, 8, tok), lower.reshape(-1, 8, tok)], axis=1)
    return both.astype(BF16)


def unweave(both):
    tok = both.shape[2]
    wide = both.astype(F32)
    upper = wide[:, :8].reshape(-1, tok).astype(BF16)
    lower = wide[:, 8:].reshape(-1, tok).astype(BF16)
    return upper, lower


def entry_kernel(tok_ref, grad_ref, left_up_ref, right_down_ref, send_ref):
    left_up_t = left_up_ref[...].astype(F32).T.astype(BF16)
    first = dot(left_up_t, tok_ref[...], NT)
    back = dot(right_down_ref[...], grad_ref[...], NT)
    send_ref[...] = weave(first, back)


def middle_kernel(recv_ref, right_up_ref, right_up_t_ref, left_down_ref, left_down_t_ref,
                  send_ref, hidden_ref, back_pre_ref, mixed_ref, back_third_ref):
    mixed, back_third = unweave(recv_ref[...])
    mixed_ref[...] = mixed
    back_third_ref[...] = back_third
    pre = dot(right_up_t_ref[...], mixed)
    back_hidden = dot(left_down_ref[...], back_third)
    square = pre * pre
    half = 0.5 + 0.5 * jnp.tanh(pre * (GELU_C + (GELU_C * GELU_A) * square))
    hidden = (pre * half).astype(BF16)
    slope = half + (half - half * half) * (pre * (2.0 * GELU_C + (6.0 * GELU_C * GELU_A) * square))
    back_pre = (back_hidden * slope).astype(BF16)
    hidden_ref[...] = hidden
    back_pre_ref[...] = back_pre
    third = dot(left_down_t_ref[...], hidden)
    back_mixed = dot(right_up_ref[...], back_pre)
    send_ref[...] = weave(third, back_mixed)


def middle_grads_kernel(place_ref, hidden_hbm, back_pre_hbm, mixed_hbm, back_third_hbm,
                        own_ref, near_ref, far_ref, last_ref,
                        hidden_ref, back_pre_ref, mixed_ref, back_third_ref, sems):
    small = [pltpu.make_async_copy(mixed_hbm, mixed_ref, sems.at[0]),
             pltpu.make_async_copy(back_third_hbm, back_third_ref, sems.at[1])]
    large = []
    for step in range(4):
        rows = pl.ds(pl.multiple_of(((place_ref[0] + step) & 3) * 256, 256), 256)
        large.append((pltpu.make_async_copy(hidden_hbm.at[rows], hidden_ref.at[step], sems.at[2 + step]),
                      pltpu.make_async_copy(back_pre_hbm.at[rows], back_pre_ref.at[step], sems.at[6 + step])))
    for copy in small:
        copy.start()
    for pair in large:
        for copy in pair:
            copy.start()
    for copy in small:
        copy.wait()
    for step, out_ref in enumerate((own_ref, near_ref, far_ref, last_ref)):
        large[step][0].wait()
        out_ref[:256] = dot(hidden_ref[step], back_third_ref[...], NT).astype(BF16)
        large[step][1].wait()
        out_ref[256:] = dot(mixed_ref[...], back_pre_ref[step], NT).astype(BF16)


def fold_kernel(place_ref, own_ref, near_ref, far_ref, last_ref, keep_ref, give_ref, total_ref):
    total_ref[...] = four_sum(own_ref[...], near_ref[...], far_ref[...], last_ref[...])
    half = place_ref[0] & 1
    keep_ref[...] = total_ref[pl.ds(pl.multiple_of(half * 256, 256), 256), :]
    give_ref[...] = total_ref[pl.ds(pl.multiple_of((1 - half) * 256, 256), 256), :]


def exit_grads_kernel(recv_ref, tok_ref, grad_ref, out_ref, mixed_ref, back_first_ref):
    mixed, back_first = unweave(recv_ref[...])
    mixed_ref[...] = mixed
    back_first_ref[...] = back_first
    out_ref[:256] = dot(mixed, grad_ref[...]).astype(BF16)
    out_ref[256:] = dot(back_first, tok_ref[...]).T.astype(BF16)


def exit_kernel(mixed_ref, back_first_ref, left_up_ref, right_down_ref, out_ref, in_grad_ref):
    left_up_t = left_up_ref[...].astype(F32).T.astype(BF16)
    out_ref[...] = dot(mixed_ref[...], right_down_ref[...], TN).astype(BF16)
    in_grad_ref[...] = dot(back_first_ref[...], left_up_t, TN).astype(BF16)


def spread_kernel(place_ref, late_ref, own_ref, other_ref, late_out_ref, early_out_ref):
    late = jnp.sum(late_ref[...].astype(F32), axis=0).astype(BF16)
    late_out_ref[...] = jnp.broadcast_to(late[None], late_out_ref.shape)
    half = place_ref[0] & 1
    early_out_ref[pl.ds(pl.multiple_of(half * 256, 256), 256), :] = own_ref[...]
    early_out_ref[pl.ds(pl.multiple_of((1 - half) * 256, 256), 256), :] = other_ref[...]


def unpack_kernel(place_ref, late_ref, own_ref, near_ref, far_ref, last_ref,
                  left_up_ref, right_up_ref, left_down_ref, right_down_ref):
    right_down_ref[...] = late_ref[:8].reshape(256, 256)
    left_up_ref[...] = late_ref[8:].reshape(256, 256)
    for step, ref in enumerate((own_ref, near_ref, far_ref, last_ref)):
        start = pl.multiple_of(((place_ref[0] + 4 - step) & 3) * 256, 256)
        left_down_ref[pl.ds(start, 256), :] = ref[:256]
        right_up_ref[:, pl.ds(start, 256)] = ref[256:]


def hbm(dims):
    return pltpu.HBM(dims, BF16)


def plain(dims):
    return jax.ShapeDtypeStruct(dims, BF16)


def in_hbm(array):
    return pltpu.with_memory_space_constraint(array, pltpu.HBM)


def along_y(array, step):
    pairs = [(z_lo * 4 + y, z_lo * 4 + (y + step) % 4) for z_lo in range(4) for y in range(4)]
    return lax.ppermute(array, "dp", pairs)


def swap_z(array, bit):
    pairs = [(z_lo * 4 + y, (z_lo ^ bit) * 4 + y) for z_lo in range(4) for y in range(4)]
    return lax.ppermute(array, "dp", pairs)


def two_sum(own, other):
    return (own.astype(F32) + other.astype(F32)).astype(BF16)


def four_sum(own, near, far, last):
    return ((own.astype(F32) + far.astype(F32)) + (near.astype(F32) + last.astype(F32))).astype(BF16)


def send_on(chunks):
    far = along_y(chunks[2], 2)
    near = along_y(chunks[1], 1)
    return [chunks[0], near, far, along_y(chunks[3], 3)]


def exchange(parts, axis):
    return lax.all_to_all(parts, axis, 0, 0, tiled=True)


def whole_call(kernel, outs, *args):
    return pl.pallas_call(kernel, out_shape=outs, compiler_params=PARAMS)(*args)


def on_device(tokens_in, out_grad, left_up, right_up, left_down, right_down):
    tok = tokens_in.shape[0]
    tile = 256
    dp_index = lax.axis_index("dp")
    y, z_lo = dp_index & 3, dp_index >> 2

    weight = lambda rows, cols: pl.BlockSpec((rows, cols), lambda i: (0, 0))
    column = lambda rows: pl.BlockSpec((rows, tile), lambda i: (0, i))
    woven = lambda cols: pl.BlockSpec((32, 16, cols), lambda i: (0, 0, i))
    half = pl.BlockSpec((tok // 2, 256), lambda i: (i, 0))
    send = pl.pallas_call(
        entry_kernel,
        grid=(2,),
        in_specs=[half, half, weight(256, 256), weight(256, 256)],
        out_specs=woven(tok // 2),
        out_shape=hbm((32, 16, tok)),
        compiler_params=PARAMS,
    )(in_hbm(tokens_in), in_hbm(out_grad), in_hbm(left_up), in_hbm(right_down))
    recv = exchange(send, "tensor")

    send, hidden, back_pre, mixed_up, back_third = pl.pallas_call(
        middle_kernel,
        grid=(tok // tile,),
        in_specs=[woven(tile), weight(256, 1024), weight(1024, 256), weight(1024, 256), weight(256, 1024)],
        out_specs=[woven(tile), column(1024), column(1024), column(256), column(256)],
        out_shape=[hbm((32, 16, tok)), hbm((1024, tok)), hbm((1024, tok)),
                   hbm((256, tok)), hbm((256, tok))],
        compiler_params=PARAMS,
    )(recv, right_up, right_up.T, left_down, left_down.T)
    recv = exchange(send, "tensor")

    vmem = pl.BlockSpec(memory_space=pltpu.VMEM)
    smem = pl.BlockSpec(memory_space=pltpu.SMEM)
    far_away = pl.BlockSpec(memory_space=pltpu.HBM)
    y_place = y.astype(jnp.int32).reshape(1)
    z_half = (z_lo >> 1).astype(jnp.int32).reshape(1)
    parts = pl.pallas_call(
        middle_grads_kernel,
        in_specs=[smem] + [far_away] * 4,
        out_shape=[plain((512, 256))] * 4,
        scratch_shapes=[pltpu.VMEM((4, 256, tok), BF16), pltpu.VMEM((4, 256, tok), BF16),
                        pltpu.VMEM((256, tok), BF16), pltpu.VMEM((256, tok), BF16),
                        pltpu.SemaphoreType.DMA((10,))],
        compiler_params=PARAMS,
    )(y_place, in_hbm(hidden), in_hbm(back_pre), in_hbm(mixed_up), in_hbm(back_third))

    keep, give = pl.pallas_call(
        fold_kernel,
        in_specs=[smem] + [vmem] * 4,
        out_shape=[plain((256, 256))] * 2,
        scratch_shapes=[pltpu.VMEM((512, 256), BF16)],
        compiler_params=PARAMS,
    )(z_half, *send_on(parts))
    part = two_sum(keep, swap_z(give, 2))
    part = two_sum(part, swap_z(part, 1))
    recv, part = lax.optimization_barrier((recv, part))
    late, mixed_down, back_first = whole_call(
        exit_grads_kernel, [hbm((512, 256)), plain((256, tok)), plain((256, tok))],
        recv, tokens_in, out_grad)

    late = exchange(late.reshape(16, 32, 256), "dp")
    late, part = pl.pallas_call(
        spread_kernel,
        in_specs=[smem] + [vmem] * 3,
        out_shape=[hbm((16, 32, 256)), plain((512, 256))],
        compiler_params=PARAMS,
    )(z_half, late, part, swap_z(part, 2))
    late = exchange(late, "dp")
    pieces = send_on([part] * 4)
    layer_out, input_grad = whole_call(
        exit_kernel, [hbm((tok, 256)), hbm((tok, 256))], mixed_down, back_first, left_up, right_down)
    grads = pl.pallas_call(
        unpack_kernel,
        in_specs=[smem] + [vmem] * 5,
        out_shape=[hbm((256, 256)), hbm((256, 1024)), hbm((1024, 256)), hbm((256, 256))],
        compiler_params=PARAMS,
    )(y_place, late, *pieces)
    return (layer_out, input_grad, *grads)


def solution(mesh):
    rows = P("tensor", None)
    return jax.shard_map(
        on_device,
        mesh=mesh,
        in_specs=(P("dp", "tensor"), P("dp", "tensor"), rows, rows, rows, rows),
        out_specs=(P("dp", "tensor"), P("dp", "tensor"), rows, rows, rows, rows),
        check_vma=False,
    )
```
